32 devices in a mesh: band: 8 (over z, x), tile: 4 (over y, core).
Axes of the slice: x: 2, y: 2, z: 4, core: 2. Of those that a mesh axis runs over, the one named last changes fastest.
Arguments:
- source: bfloat16 [40, 262144], P(None, ('band', 'tile')), may hold values from -6 to 6
- regrid_weights: bfloat16 [2048, 4, 128, 128], P(('band', 'tile')), may hold values from -0.5 to 0.5
- dest_group: int32 [2048, 4], P(('band', 'tile')), may hold values from 0 to 31, all different within a row; in each aligned block of 64 rows (0 to 63, 64 to 127, ...) at most 24 rows name the same one
- dest_block: int32 [2048, 4], P(('band', 'tile')), may hold values from 0 to 767
- seam_table: int32 [12, 4, 3], replicated, may hold values from 0 to 11, as said below
- conv1_weight: bfloat16 [9, 128, 40], replicated, may hold values from -0.3125 to 0.3125
- conv1_bias: float32 [128], replicated, may hold values from -3 to 3
- conv2_weight: bfloat16 [9, 128, 128], replicated, may hold values from -0.1875 to 0.1875
- conv2_bias: float32 [128], replicated, may hold values from -3 to 3
Outputs:
- features: bfloat16 [128, 12, 512, 512], P(None, None, 'band', 'tile')
The draws below stay inside these ranges and needn't reach their ends.
Inputs may be any that keep to these rules, and one draw needn't show every extreme that they name: `dest_group`: within the rows of one device (aligned blocks of 64 rows) no value appears more than 24 times, and a row's 4 values differ. `seam_table`: entries 0 and 1 name a face and a side (0 to 3). Joins are symmetric: if side s of face f is joined to side s2 of face g, side s2 of face g is joined to side s of face f with the same reversal entry. No side is joined to itself. Entry 2 is 0 or 1.
All inputs are finite; a program needn't handle non-finite values.
Results may differ from the reference program's by a relative error of at most 0.0058.
Values may be sent and summed in bfloat16 or wider, within the bound.
A program may use at most 640 MiB of HBM per device.

```python
import math
import jax
import jax.numpy as jnp
import numpy as np
from jax import lax

FIELDS = 40
HID = 128
BLK = 128
FACES = 12
KB = 4
SB_DEV = 64
C = 24
NSIDE = 512
ROWS_DEV = 64
TB_DEV = 768
SRC_BLOCKS = 2048
SRC_CELLS = 262144
N_BAND = 8
N_TILE = 4
DEVICES = 32


def draw_seam_table(key, part):
    order = jax.random.permutation(key, 4 * FACES).astype(jnp.int32)
    firsts = order[0::2]
    seconds = order[1::2]
    partner = jnp.zeros((4 * FACES,), jnp.int32).at[firsts].set(seconds).at[seconds].set(firsts)
    flips = jax.random.randint(jax.random.fold_in(key, 7), (2 * FACES,), 0, 2).astype(jnp.int32)
    reverse = jnp.zeros((4 * FACES,), jnp.int32).at[firsts].set(flips).at[seconds].set(flips)
    return jnp.stack((partner // 4, partner % 4, reverse), axis=1).reshape(FACES, 4, 3).astype(jnp.int32)


def with_ends(values, own_key, low, high):
    extent = values.shape
    place = [jax.random.randint(jax.random.fold_in(own_key, axis), (), 0, extent[axis]) for axis in range(len(extent))]
    values = values.at[tuple(place)].set(low)
    longest = extent.index(max(extent))
    place[longest] = (place[longest] + 1) % extent[longest]
    return values.at[tuple(place)].set(high)


def block_scale(own_key, extent, pieces, smallest, largest):
    loudness = 1.0
    for position, shards_of in pieces:
        heights = jax.random.uniform(jax.random.fold_in(jax.random.fold_in(own_key, 6), position), (shards_of,), jnp.float32, smallest / len(pieces), largest / len(pieces))
        loudness = loudness * jnp.repeat(jnp.exp(heights), extent[position] // shards_of).reshape((-1,) + (1,) * (len(extent) - 1 - position))
    return loudness


def routed_block(rng, own, number, rows, number_of, top, limit, lean):
    sequence = jax.random.permutation(rng, number_of)
    heavy_load, common = portions_of(number_of, rows * top, limit, lean, True), portions_of(number_of, rows * top, limit, lean, False)
    places = jnp.arange(number_of)

    def named(sizes, turn):
        used = int((sizes > 0).sum())
        fixed = max(1, used // 4)
        shifted = fixed + (places - fixed + turn * (used - fixed)) % max(1, number_of - fixed)
        return jnp.zeros((number_of,), jnp.int32).at[sequence[jnp.where(places < fixed, places, shifted)]].set(jnp.asarray(sizes, jnp.int32))

    sizes = jnp.where(number % 4 == 0, named(heavy_load, number // 4), named(common, number - number // 4 - 1))
    mixed = jax.random.permutation(jax.random.fold_in(own, 3), number_of)
    source_of, taker = mixed[0:number_of // 2 * 2:2], mixed[1:number_of // 2 * 2:2]
    room = jnp.minimum(sizes[source_of] - 1, limit - sizes[taker]) // 2
    room = jnp.where((source_of == sequence[0]) | (taker == sequence[0]) | (sizes[taker] == 0), 0, jnp.maximum(room, 0))
    shifted = jax.random.randint(jax.random.fold_in(own, 4), (number_of // 2,), 0, 1 << 20) % (room + 1)
    sizes = sizes.at[source_of].add(-shifted).at[taker].add(shifted)
    items = jnp.searchsorted(jnp.cumsum(sizes), jnp.arange(rows * top), side="right").astype(jnp.int32)
    listing = items.reshape(top, rows).T
    listing = listing[jax.random.permutation(jax.random.fold_in(own, 1), rows)]
    turn = jax.random.randint(jax.random.fold_in(own, 2), (rows, 1), 0, top)
    return jnp.take_along_axis(listing, (jnp.arange(top)[None, :] + turn) % top, axis=1)


def portions_of(amount, total, limit, slope, full):
    portions = [(1 << 20) // math.isqrt(rank ** slope) + 1 for rank in range(1, amount + 1)]
    largest = limit if full else min(limit, max(-(-total // amount), total * portions[0] // sum(portions)))
    least = 1 if total - largest >= amount - 1 else 0
    holding, spare = [largest] + [least] * (amount - 1), total - largest - least * (amount - 1)
    while spare > 0:
        candidates = [i for i in range(1, amount) if holding[i] < largest] or [i for i in range(1, amount) if holding[i] < limit]
        pool, remaining = sum([portions[i] for i in candidates]), spare
        for i in candidates:
            addition = min(limit - holding[i], max(1, remaining * portions[i] // pool), spare)
            holding[i] = holding[i] + addition
            spare = spare - addition
    return np.array(holding)


def noise(rng, dims, scale, reach, pieces=(), held_as=jnp.bfloat16):
    entries = jax.random.normal(rng, dims, jnp.float32) * scale
    if len(pieces) > 0:
        entries = block_scale(rng, dims, pieces, -0.22, 0.18) * entries
    return jnp.clip(entries, min=-reach, max=reach).astype(held_as)


def setup_inputs(seed: int = 0) -> dict:
    seeds = jax.random.split(jax.random.key(seed), 10)
    source = noise(seeds[0], (FIELDS, SRC_CELLS), 1.0, 6.0, ((1, 32),))
    regrid_weights = noise(seeds[1], (SRC_BLOCKS, KB, BLK, BLK), BLK ** -0.5, 0.5, ((0, 32),))
    dest_group_keys = jax.random.split(jax.random.fold_in(seeds[2], 1), SRC_BLOCKS // SB_DEV)
    dest_group_turns = jax.random.permutation(jax.random.fold_in(seeds[2], 3), SRC_BLOCKS // SB_DEV)
    dest_group = jax.vmap(lambda own, number: routed_block(jax.random.fold_in(seeds[2], 2), own, number, SB_DEV, DEVICES, KB, C, 1))(dest_group_keys, dest_group_turns).reshape((SRC_BLOCKS, KB))
    dest_block = with_ends(jax.random.randint(seeds[3], (SRC_BLOCKS, KB), 0, TB_DEV), jax.random.fold_in(seeds[3], 1), 0, TB_DEV - 1).astype(jnp.int32)
    seam_table = draw_seam_table(jax.random.fold_in(seeds[9], 71), 0)
    conv1_weight = noise(seeds[5], (9, HID, FIELDS), (9 * FIELDS) ** -0.5, 0.3125)
    conv1_bias = noise(seeds[6], (HID,), 0.5, 3.0, (), jnp.float32)
    conv2_weight = noise(seeds[7], (9, HID, HID), (9 * HID) ** -0.5, 0.1875)
    conv2_bias = noise(seeds[8], (HID,), 0.5, 3.0, (), jnp.float32)
    return dict(source=source, regrid_weights=regrid_weights, dest_group=dest_group, dest_block=dest_block, seam_table=seam_table, conv1_weight=conv1_weight, conv1_bias=conv1_bias, conv2_weight=conv2_weight, conv2_bias=conv2_bias)


def conv_faces(field_in, weight, bias_row, seam_table):
    channels = field_in.shape[0]
    side_len = field_in.shape[2]
    edge_lines = jnp.stack((field_in[:, :, 0, :], field_in[:, :, -1, :], field_in[:, :, :, 0], field_in[:, :, :, -1]), axis=2).reshape(channels, FACES * 4, side_len)
    line_index = (seam_table[:, :, 0] * 4 + seam_table[:, :, 1]).reshape(-1)
    reverse = (seam_table[:, :, 2] == 1).reshape(-1)[None, :, None]
    seam_lines = edge_lines[:, line_index, :]
    seam_lines = jnp.where(reverse, jnp.flip(seam_lines, axis=2), seam_lines).reshape(channels, FACES, 4, side_len)
    weight_wide = weight.astype(jnp.float32)

    def one_face(face_id):
        face_data = field_in[:, face_id]
        face_lines = seam_lines[:, face_id]
        padded = jnp.pad(face_data, ((0, 0), (1, 1), (1, 1)))
        padded = padded.at[:, 0, 1:-1].set(face_lines[:, 0])
        padded = padded.at[:, -1, 1:-1].set(face_lines[:, 1])
        padded = padded.at[:, 1:-1, 0].set(face_lines[:, 2])
        padded = padded.at[:, 1:-1, -1].set(face_lines[:, 3])
        padded = padded.astype(jnp.float32)
        summed = jnp.zeros((weight.shape[1], side_len, side_len), jnp.float32)
        for row_off in range(3):
            for col_off in range(3):
                window = padded[:, row_off:row_off + side_len, col_off:col_off + side_len]
                summed = summed + jnp.einsum("oi,irc->orc", weight_wide[3 * row_off + col_off], window)
        return jax.nn.gelu(summed + bias_row[:, None, None], approximate=False).astype(jnp.bfloat16)

    out_faces = lax.map(one_face, jnp.arange(FACES, dtype=jnp.int32))
    return jnp.transpose(out_faces, (1, 0, 2, 3))


def reference(source, regrid_weights, dest_group, dest_block, seam_table, conv1_weight, conv1_bias, conv2_weight, conv2_bias):
    devices = N_BAND * N_TILE
    group_blocks = source.reshape(FIELDS, devices, SB_DEV, BLK).transpose(1, 2, 0, 3)
    group_weights = regrid_weights.reshape(devices, SB_DEV, KB, BLK, BLK)

    def one_group(group_pair):
        blocks, weights = group_pair
        return jnp.einsum("sfc,skcd->skfd", blocks.astype(jnp.float32), weights.astype(jnp.float32)).astype(jnp.bfloat16)

    partial_value = lax.map(one_group, (group_blocks, group_weights))
    target = (dest_group * TB_DEV + dest_block).reshape(-1).astype(jnp.int32)
    summed = jax.ops.segment_sum(partial_value.reshape(-1, FIELDS, BLK).astype(jnp.float32), target, num_segments=devices * TB_DEV)
    regridded = summed.reshape(N_BAND, N_TILE, FACES, ROWS_DEV, FIELDS, BLK).transpose(4, 2, 0, 3, 1, 5).reshape(FIELDS, FACES, NSIDE, NSIDE).astype(jnp.bfloat16)
    hidden = conv_faces(regridded, conv1_weight, conv1_bias, seam_table)
    return conv_faces(hidden, conv2_weight, conv2_bias, seam_table)
```

```python
import functools

import jax
import jax.numpy as jnp
from jax import lax
from jax.experimental import pallas as pl
from jax.experimental.pallas import tpu as pltpu
from jax.sharding import PartitionSpec as P

BF = jnp.bfloat16
F32 = jnp.float32
VMEM_LIMIT = 60 * 1024 * 1024
PAIRS = 8
UNROLLED = True
CH = 16
MESH = pl.DeviceIdType.MESH
GELU_COEF = (
    0.7978842684146765,
    0.03633414911622174,
    -3.30267008968913e-05,
    -5.527338755532785e-05,
    3.974071022505988e-06,
    -1.3378322650770525e-07,
    1.8139281733930472e-09,
)
GELU_CAP = 30.0


def gelu(v):
    u = jnp.minimum(v * v, GELU_CAP)
    q = jnp.full_like(u, GELU_COEF[-1])
    for c in GELU_COEF[-2::-1]:
        q = q * u + c
    half = 0.5 * v
    return half + half * jnp.tanh(v * q)


def partial_kernel(pos_ref, src_ref, w_ref, out_ref):
    s = pl.program_id(0)
    per_step = w_ref.shape[0]
    top, blk = w_ref.shape[1], w_ref.shape[2]

    @pl.when(s == 0)
    def _():
        out_ref[...] = jnp.zeros_like(out_ref)

    for j in range(per_step):
        x = src_ref[:, j * blk : (j + 1) * blk]
        for k in range(top):
            y = jnp.dot(x, w_ref[j, k], preferred_element_type=F32).astype(BF)
            out_ref[pos_ref[(s * per_step + j) * top + k]] = y


def partials(position, source, weights, slots):
    fields = source.shape[0]
    src_count, top, blk, _ = weights.shape
    step = 4
    return pl.pallas_call(
        partial_kernel,
        out_shape=jax.ShapeDtypeStruct((slots, fields, blk), BF),
        grid_spec=pltpu.PrefetchScalarGridSpec(
            num_scalar_prefetch=1,
            grid=(src_count // step,),
            in_specs=[
                pl.BlockSpec((fields, step * blk), lambda i, p: (0, i)),
                pl.BlockSpec((step, top, blk, blk), lambda i, p: (i, 0, 0, 0)),
            ],
            out_specs=pl.BlockSpec((slots, fields, blk), lambda i, p: (0, 0, 0)),
        ),
        compiler_params=pltpu.CompilerParams(vmem_limit_bytes=VMEM_LIMIT),
        name="partials",
    )(position, source, weights)


def collect_kernel(slot_ref, arr_ref, out_ref, acc_ref):
    i = pl.program_id(0)
    n = arr_ref.shape[0]

    @pl.when(i == 0)
    def _():
        acc_ref[...] = jnp.zeros_like(acc_ref)

    def body(j, _):
        slot = slot_ref[i * n + j]
        acc_ref[slot] = acc_ref[slot] + arr_ref[j].astype(F32)
        return 0

    lax.fori_loop(0, n, body, 0, unroll=4)

    @pl.when(i == pl.num_programs(0) - 1)
    def _():
        out_ref[...] = acc_ref[: out_ref.shape[0]].astype(BF)


def collect(slots, arrived, slots_dev):
    count, fields, blk = arrived.shape
    steps = 8
    return pl.pallas_call(
        collect_kernel,
        out_shape=jax.ShapeDtypeStruct((slots_dev, fields, blk), BF),
        grid_spec=pltpu.PrefetchScalarGridSpec(
            num_scalar_prefetch=1,
            grid=(steps,),
            in_specs=[pl.BlockSpec((count // steps, fields, blk), lambda i, p: (i, 0, 0))],
            out_specs=pl.BlockSpec((slots_dev, fields, blk), lambda i, p: (0, 0, 0)),
            scratch_shapes=[pltpu.VMEM((slots_dev + 1, fields, blk), F32)],
        ),
        compiler_params=pltpu.CompilerParams(vmem_limit_bytes=VMEM_LIMIT),
        name="collect",
    )(slots, arrived)


def conv_kernel(
    first, x_ref, top_ref, bot_ref, left_ref, right_ref, wa_ref, wb_ref, b_ref, out_ref, *scratch
):
    if first:
        ends_ref, ends = scratch[0], scratch[-1]
        scratch = scratch[1:]
    sl, win, side = scratch[0], scratch[1], scratch[2]
    rows = out_ref.shape[0] if first else out_ref.shape[2]
    cols = sl.shape[1]
    width = sl.shape[2] // 2
    chan = x_ref.shape[1]
    slots = win.shape[0]
    side[0] = left_ref[0, CH : CH + rows, :].astype(F32)
    side[1] = right_ref[0, CH : CH + rows, :].astype(F32)

    def put(slot, pair, parity, row32, lo, hi):
        win[slot, 8 : 8 + cols, :] = row32
        win[slot, 7:8, :] = lo
        win[slot, 8 + cols : 9 + cols, :] = hi
        before = win[slot, 7 : 7 + cols, :]
        after = win[slot, 9 : 9 + cols, :]
        base = parity * width
        if first:
            g = before + pltpu.roll(row32, chan, 1) + pltpu.roll(after, 2 * chan, 1)
            sl[pair, :, base : base + width] = g.astype(BF)
        else:
            sl[pair, :, base : base + cols] = before.astype(BF)
            sl[pair, :, base + cols : base + 2 * cols] = row32.astype(BF)
            sl[pair, :, base + 2 * cols : base + 3 * cols] = after.astype(BF)

    def row_at(r):
        if first:
            y = x_ref[r].astype(F32)
            y = jnp.concatenate([y, jnp.zeros((cols - chan, cols), F32)], axis=0)
            return y.T
        return x_ref[r].astype(F32)

    def halo_row(ref):
        full = ref[0].astype(F32)
        return full[CH : CH + cols], full[CH - 1 : CH], full[CH + cols : CH + cols + 1]

    def put_row(r, k):
        put(
            k % slots,
            r // 2 + k % 2 if isinstance(r, int) else (r - k % 2) // 2 + k % 2,
            1 - k % 2,
            row_at(r),
            side[0, pl.ds(r, 1), :],
            side[1, pl.ds(r, 1), :],
        )

    row, lo, hi = halo_row(top_ref)
    put(0, 0, 0, row, lo, hi)
    row, lo, hi = halo_row(bot_ref)
    put(1, rows // 2, 1, row, lo, hi)
    unroll = UNROLLED
    n = 2 * PAIRS

    def fill_loop(i, _):
        for k in range(slots):
            put_row(i * slots + k, k)
        return 0

    def dots(p0):
        a = sl[pl.ds(p0, PAIRS)].reshape(PAIRS * cols, 2 * width)
        b = sl[pl.ds(p0 + 1, PAIRS)].reshape(PAIRS * cols, 2 * width)
        return jnp.dot(a, wa_ref[...], preferred_element_type=F32) + jnp.dot(
            b, wb_ref[...], preferred_element_type=F32
        )

    def finish(g, y):
        p0 = g * PAIRS
        hid = y.shape[1] // 2
        if first:
            y = gelu(y + b_ref[...])
            for p in range(PAIRS):
                for q in range(2):
                    part = y[p * cols : (p + 1) * cols, q * hid : (q + 1) * hid].astype(BF)
                    r = 2 * (p0 + p) + q
                    out_ref[r] = part
                    ends[0, pl.ds(r, 1), :] = part[:1].astype(F32)
                    ends[1, pl.ds(r, 1), :] = part[cols - 1 :].astype(F32)
            return
        flip = scratch[3].at[g % 2 if unroll else 0]
        for p in range(PAIRS):
            for q in range(2):
                part = y[p * cols : (p + 1) * cols, q * hid : (q + 1) * hid]
                flip[pl.ds(2 * p + q, hid, stride=n), :] = part.T

        def group(o, _):
            for j in range(8):
                v = flip[pl.ds((o * 8 + j) * n, n), :]
                out_ref[o * 8 + j, 0, pl.ds(g * n, n), :] = gelu(v + b_ref[o * 8 + j]).astype(BF)
            return 0

        if unroll:
            for o in range(hid // 8):
                group(o, 0)
        else:
            lax.fori_loop(0, hid // 8, group, 0)

    if unroll:
        for k in range(min(n + 2, rows)):
            put_row(k, k)
        for g in range(rows // n):
            y = dots(g * PAIRS)
            for k in range((g + 1) * n + 2, min((g + 2) * n + 2, rows)):
                put_row(k, k)
            finish(g, y)
    else:
        lax.fori_loop(0, rows // slots, fill_loop, 0)

        def chunk(g, _):
            finish(g, dots(g * PAIRS))
            return 0

        lax.fori_loop(0, rows // n, chunk, 0)
    if first:
        ends_ref[:, 0] = ends[...].astype(BF)


def conv(first, x, halos, weight, bias, face_count, rows, out_cols):
    top, bot, left, right = halos
    hid, chan = weight.shape[1], weight.shape[2]
    cols = out_cols
    w = weight.reshape(3, 3, hid, chan).transpose(0, 1, 3, 2)
    if first:
        w = w.reshape(3, 3 * chan, hid)
        w = jnp.pad(w, ((0, 0), (0, cols - 3 * chan), (0, 0)))
    else:
        w = w.reshape(3, 3 * chan, hid)
    width = w.shape[1]
    zero = jnp.zeros((width, hid), w.dtype)
    wide = [
        jnp.concatenate([w[a] if a < 3 else zero, w[a - 1] if a > 0 else zero], axis=1)
        for a in range(4)
    ]
    wa = jnp.concatenate(wide[:2], axis=0)
    wb = jnp.concatenate(wide[2:], axis=0)
    scratch = [
        pltpu.VMEM((rows // 2 + 1, cols, 2 * width), BF),
        pltpu.VMEM((8, cols + 16, cols), F32),
        pltpu.VMEM((2, rows, cols), F32),
    ]
    if first:
        bias_in = jnp.concatenate([bias, bias])[None, :]
        bias_spec = pl.BlockSpec((1, 2 * hid), lambda f: (0, 0))
        out_shape = (
            jax.ShapeDtypeStruct((face_count * rows, cols, hid), BF),
            jax.ShapeDtypeStruct((2, face_count, rows, hid), BF),
        )
        out_spec = (
            pl.BlockSpec((rows, cols, hid), lambda f: (f, 0, 0)),
            pl.BlockSpec((2, 1, rows, hid), lambda f: (0, f, 0, 0)),
        )
        scratch.append(pltpu.VMEM((2, rows, hid), F32))
    else:
        bias_in = bias
        bias_spec = pl.BlockSpec(memory_space=pltpu.SMEM)
        out_shape = jax.ShapeDtypeStruct((hid, face_count, rows, cols), BF)
        out_spec = pl.BlockSpec((hid, 1, rows, cols), lambda f: (0, f, 0, 0))
        scratch.append(pltpu.VMEM((2, hid * 2 * PAIRS, cols), F32))
    return pl.pallas_call(
        functools.partial(conv_kernel, first),
        out_shape=out_shape,
        grid=(face_count,),
        in_specs=[
            pl.BlockSpec((rows,) + x.shape[1:], lambda f: (f, 0, 0)),
            pl.BlockSpec((1,) + top.shape[1:], lambda f: (f, 0, 0)),
            pl.BlockSpec((1,) + bot.shape[1:], lambda f: (f, 0, 0)),
            pl.BlockSpec((1,) + left.shape[1:], lambda f: (f, 0, 0)),
            pl.BlockSpec((1,) + right.shape[1:], lambda f: (f, 0, 0)),
            pl.BlockSpec(wa.shape, lambda f: (0, 0)),
            pl.BlockSpec(wb.shape, lambda f: (0, 0)),
            bias_spec,
        ],
        out_specs=out_spec,
        scratch_shapes=scratch,
        compiler_params=pltpu.CompilerParams(vmem_limit_bytes=VMEM_LIMIT),
        name="conv1" if first else "conv2",
    )(x, top, bot, left, right, wa, wb, bias_in)


def halo_kernel(line_refs, nb, nt, tab_ref, *refs):
    ins, refs = refs[:line_refs], refs[line_refs:]
    tops, bots, lefts, rights, cand, pick, recv, send, met = refs
    faces, rows, cols = tops.shape[0], lefts.shape[1] - 2 * CH, tops.shape[1] - 2 * CH
    if line_refs == 2:
        top, bot = ins[0].at[:, 0], ins[0].at[:, rows - 1]
        left, right = ins[1].at[0], ins[1].at[1]
    else:
        top, bot, left, right = ins
    b, t = lax.axis_index("band"), lax.axis_index("tile")
    me = b * nt + t
    per_col, per_row = rows // CH, cols // CH
    chunks = nt * per_row
    classes = chunks // 2
    step = nb * nt // classes
    both = jnp.logical_and
    last_b, last_t = b == nb - 1, t == nt - 1
    TOP, BOT, LEFT, RIGHT = 0, 3, 6, 9
    main, lead = pl.ds(CH, cols), pl.ds(0, CH)
    main_v, trail_v = pl.ds(CH, rows), pl.ds(CH + rows, CH)
    trail = pl.ds(CH + cols, CH)
    started = []

    def go(cond, src, dst, sem, db, dt, own=True):
        same = db * nt + dt == me
        copy = pltpu.make_async_remote_copy(
            src_ref=src, dst_ref=dst, send_sem=send.at[len(started)], recv_sem=sem,
            device_id=(db, dt), device_id_type=MESH,
        )
        away = both(cond, jnp.logical_not(same)) if own else cond
        pl.when(away)(copy.start)
        if own:
            pl.when(both(cond, same))(pltpu.make_async_copy(src, dst, sem).start)
        started.append((away, copy))

    def taken(cond, ref, sem):
        pl.when(cond)(pltpu.make_async_copy(ref, ref, sem).wait)

    lines = [
        (b == 0, top, t * per_row, per_row),
        (last_b, bot, t * per_row, per_row),
        (t == 0, left, b * per_col, per_col),
        (last_t, right, b * per_col, per_col),
    ]
    for side, (cond, line, first, count) in enumerate(lines):
        for i in range(count):
            k = first + i
            upper = k // classes
            at = (k + upper * (chunks - 1 - 2 * k)) * step
            go(cond, line.at[:, pl.ds(i * CH, CH)], cand.at[upper, side], met, at // nt, at % nt)
    for cond, line, dst, base, db in (
        (b > 0, top, bots, BOT, b - 1),
        (b < nb - 1, bot, tops, TOP, b + 1),
    ):
        go(cond, line, dst.at[:, main], recv.at[base], db, t, False)
        go(both(cond, t > 0), line.at[:, pl.ds(0, CH)], dst.at[:, trail], recv.at[base + 2],
           db, t - 1, False)
        go(both(cond, t < nt - 1), line.at[:, pl.ds(cols - CH, CH)], dst.at[:, lead],
           recv.at[base + 1], db, t + 1, False)
    go(t > 0, left, rights.at[:, main_v], recv.at[RIGHT], b, t - 1, False)
    go(t < nt - 1, right, lefts.at[:, main_v], recv.at[LEFT], b, t + 1, False)

    meets = both(me % step == 0, me // step < classes)
    taken(meets, cand, met)
    near = lax.broadcasted_iota(jnp.int32, (CH, CH), 0)
    far = lax.broadcasted_iota(jnp.int32, (CH, CH), 1)
    mirror = jnp.where(near + far == CH - 1, 1.0, 0.0).astype(BF)

    @pl.when(meets)
    def _():
        def choose(f, _):
            for side in range(4):
                e = (f * 4 + side) * 3
                face, edge, rev = tab_ref[e], tab_ref[e + 1], tab_ref[e + 2]
                for h in range(2):
                    turned = jnp.dot(mirror, cand[1 - h, edge, face], preferred_element_type=F32)
                    pick[h, side, f] = jnp.where(
                        rev == 1, turned, cand[h, edge, face].astype(F32)
                    ).astype(BF)
            return 0

        lax.fori_loop(0, faces, choose, 0)

    low = me // step
    for h in range(2):
        k = low if h == 0 else chunks - 1 - low
        for side in range(4):
            src = pick.at[h, side]
            if side < 2:
                owner, off = k // per_row, k % per_row
                dst, base, db = ((tops, TOP, 0), (bots, BOT, nb - 1))[side]
                size, per, ends, length = nt, per_row, (lead, trail), cols
                dev = lambda o: (db, o)
            else:
                owner, off = k // per_col, k % per_col
                dst, base, dt = ((lefts, LEFT, 0), (rights, RIGHT, nt - 1))[side - 2]
                size, per, ends, length = nb, per_col, (lead, trail_v), rows
                dev = lambda o: (o, dt)
            go(meets, src, dst.at[:, pl.ds(CH + off * CH, CH)], recv.at[base], *dev(owner))
            go(both(meets, both(off == per - 1, owner < size - 1)), src, dst.at[:, ends[0]],
               recv.at[base + 1], *dev(owner + 1))
            go(both(meets, both(off == 0, owner > 0)), src, dst.at[:, ends[1]],
               recv.at[base + 2], *dev(owner - 1))

    for dst, base in ((tops, TOP), (bots, BOT)):
        taken(me >= 0, dst.at[:, main], recv.at[base])
        taken(t > 0, dst.at[:, lead], recv.at[base + 1])
        taken(t < nt - 1, dst.at[:, trail], recv.at[base + 2])
    for dst, base, cond in ((lefts, LEFT, t == 0), (rights, RIGHT, last_t)):
        taken(me >= 0, dst.at[:, main_v], recv.at[base])
        taken(both(cond, b > 0), dst.at[:, lead], recv.at[base + 1])
        taken(both(cond, b < nb - 1), dst.at[:, trail_v], recv.at[base + 2])

    for cond, src, end in ((t == 0, lefts, lead), (last_t, rights, trail)):
        for present, dst, part, row in (
            (b > 0, tops, lead, CH - 1),
            (b < nb - 1, bots, trail_v, 0),
        ):
            turn = ((CH - 1 if end is lead else 0) - row) % CH

            @pl.when(both(cond, present))
            def _():
                def corner(f, _):
                    v = src[f, part, :].astype(F32)
                    dst[f, end, :] = (pltpu.roll(v, turn, 0) if turn else v).astype(BF)
                    return 0

                lax.fori_loop(0, faces, corner, 0)

            @pl.when(both(cond, jnp.logical_not(present)))
            def _():
                dst[:, end, :] = jnp.zeros((faces, CH, dst.shape[2]), BF)

    for away, copy in started:
        pl.when(away)(copy.wait_send)


def halo_exchange(lines, seam_table, rows, cols, name):
    nb, nt = lax.axis_size("band"), lax.axis_size("tile")
    faces, chan = seam_table.shape[0], lines[0].shape[-1]
    per_col, per_row = rows // CH, cols // CH
    sends = 2 * per_col + 2 * per_row + 8 + 24
    row_line = jax.ShapeDtypeStruct((faces, cols + 2 * CH, chan), BF)
    col_line = jax.ShapeDtypeStruct((faces, rows + 2 * CH, chan), BF)
    vmem = pl.BlockSpec(memory_space=pltpu.VMEM)
    return pl.pallas_call(
        functools.partial(halo_kernel, len(lines), nb, nt),
        out_shape=(row_line, row_line, col_line, col_line),
        in_specs=[pl.BlockSpec(memory_space=pltpu.SMEM)]
        + [pl.BlockSpec(memory_space=pl.ANY)] * len(lines),
        out_specs=(vmem,) * 4,
        scratch_shapes=[
            pltpu.VMEM((2, 4, faces, CH, chan), BF),
            pltpu.VMEM((2, 4, faces, CH, chan), BF),
            pltpu.SemaphoreType.DMA((12,)),
            pltpu.SemaphoreType.DMA((sends,)),
            pltpu.SemaphoreType.DMA,
        ],
        compiler_params=pltpu.CompilerParams(has_side_effects=True),
        name=name,
    )(seam_table.reshape(-1), *lines)


def local(
    source,
    regrid_weights,
    dest_group,
    dest_block,
    seam_table,
    conv1_weight,
    conv1_bias,
    conv2_weight,
    conv2_bias,
):
    fields = source.shape[0]
    src_count, top_count, block_len, _ = regrid_weights.shape
    nb, nt = lax.axis_size("band"), lax.axis_size("tile")
    devices = nb * nt
    capacity = 3 * src_count * top_count // devices
    rows = block_len * nt // nb
    faces = seam_table.shape[0]
    slots_dev = faces * rows
    items = src_count * top_count
    target_dev = dest_group.reshape(items)
    target_slot = dest_block.reshape(items)
    onehot = (target_dev[:, None] == jnp.arange(devices, dtype=jnp.int32)[None, :]).astype(F32)
    earlier = (jnp.arange(items)[:, None] > jnp.arange(items)[None, :]).astype(BF)
    before = jnp.dot(earlier, onehot.astype(BF), preferred_element_type=F32)
    rank_in = jnp.sum(before * onehot, axis=1).astype(jnp.int32)
    position = target_dev * capacity + rank_in
    hit = position[None, :] == jnp.arange(devices * capacity, dtype=jnp.int32)[:, None]
    out_slots = slots_dev + jnp.sum(jnp.where(hit, target_slot[None, :] - slots_dev, 0), axis=1)
    outgoing = partials(position, source, regrid_weights, devices * capacity)
    axes = ("band", "tile")
    arrived = lax.all_to_all(
        outgoing.reshape(devices, capacity, fields, block_len), axes, 0, 0, tiled=True
    )
    arrived_slots = lax.all_to_all(
        out_slots.reshape(devices, capacity), axes, 0, 0, tiled=True
    )
    grid = collect(
        arrived_slots.reshape(-1), arrived.reshape(devices * capacity, fields, block_len), slots_dev
    )
    tiles = grid.reshape(faces, rows, fields, block_len)
    pick = jnp.eye(block_len, dtype=BF)[jnp.array([0, block_len - 1])]
    ends = jnp.einsum("ep,tcp->etc", pick, grid, preferred_element_type=F32).astype(BF)
    ends = ends.reshape(2, faces, rows, fields)
    spare = ((0, 0), (0, 0), (0, block_len - fields))
    lines = [
        jnp.pad(tiles[:, 0].transpose(0, 2, 1), spare),
        jnp.pad(tiles[:, -1].transpose(0, 2, 1), spare),
        jnp.pad(ends[0], spare),
        jnp.pad(ends[1], spare),
    ]
    halos = halo_exchange(lines, seam_table, rows, block_len, "halo1")
    hidden, ends = conv(True, grid, halos, conv1_weight, conv1_bias, faces, rows, block_len)
    tiles = hidden.reshape(faces, rows, block_len, hidden.shape[2])
    halos = halo_exchange([tiles, ends], seam_table, rows, block_len, "halo2")
    return conv(False, hidden, halos, conv2_weight, conv2_bias, faces, rows, block_len)


def solution(mesh):
    return jax.shard_map(
        local,
        mesh=mesh,
        in_specs=(
            P(None, ("band", "tile")),
            P(("band", "tile"), None, None, None),
            P(("band", "tile"), None),
            P(("band", "tile"), None),
            P(),
            P(),
            P(),
            P(),
            P(),
        ),
        out_specs=P(None, None, "band", "tile"),
        check_vma=False,
    )
```

```python
import functools

import jax
import jax.numpy as jnp
from jax import lax
from jax.experimental import pallas as pl
from jax.experimental.pallas import tpu as pltpu
from jax.sharding import PartitionSpec as P

BF = jnp.bfloat16
F32 = jnp.float32
VMEM_LIMIT = 60 * 1024 * 1024
PAIRS = 8
UNROLLED = True
CH = 16
PLANES = 4
ROUNDS = 2
FAR_ORDER = (2, 1, 3)
MESH = pl.DeviceIdType.MESH
GELU_COEF = (
    0.7978842684146765,
    0.03633414911622174,
    -3.30267008968913e-05,
    -5.527338755532785e-05,
    3.974071022505988e-06,
    -1.3378322650770525e-07,
    1.8139281733930472e-09,
)
GELU_CAP = 30.0


def gelu(v):
    u = jnp.minimum(v * v, GELU_CAP)
    q = jnp.full_like(u, GELU_COEF[-1])
    for c in GELU_COEF[-2::-1]:
        q = q * u + c
    half = 0.5 * v
    return half + half * jnp.tanh(v * q)


def partial_kernel(pos_ref, src_ref, w_ref, out_ref):
    s = pl.program_id(0)
    per_step = w_ref.shape[0]
    top, blk = w_ref.shape[1], w_ref.shape[2]

    @pl.when(s == 0)
    def _():
        out_ref[...] = jnp.zeros_like(out_ref)

    for j in range(per_step):
        x = src_ref[:, j * blk : (j + 1) * blk]
        for k in range(top):
            y = jnp.dot(x, w_ref[j, k], preferred_element_type=F32).astype(BF)
            out_ref[pos_ref[(s * per_step + j) * top + k]] = y


def partials(position, source, weights, slots):
    fields = source.shape[0]
    src_count, top, blk, _ = weights.shape
    step = 4
    return pl.pallas_call(
        partial_kernel,
        out_shape=jax.ShapeDtypeStruct((slots, fields, blk), BF),
        grid_spec=pltpu.PrefetchScalarGridSpec(
            num_scalar_prefetch=1,
            grid=(src_count // step,),
            in_specs=[
                pl.BlockSpec((fields, step * blk), lambda i, p: (0, i)),
                pl.BlockSpec((step, top, blk, blk), lambda i, p: (i, 0, 0, 0)),
            ],
            out_specs=pl.BlockSpec((slots, fields, blk), lambda i, p: (0, 0, 0)),
        ),
        compiler_params=pltpu.CompilerParams(vmem_limit_bytes=VMEM_LIMIT),
        name="partials",
    )(position, source, weights)


def route_kernel(caps, nb, nt, start_ref, out_ref, arr, *scratch):
    kept = len(caps) * PLANES
    packed, far_sem, near_sem, send_far, send_near = scratch[kept:]
    held = [scratch[r * PLANES : (r + 1) * PLANES] for r in range(len(caps))]
    members, each = packed.shape[2], packed.shape[3]
    me = lax.axis_index("band") * nt + lax.axis_index("tile")
    plane, place = me // members, me % members

    def far_copy(r, off):
        other = (plane + off) % PLANES
        to = other * members + place
        return pltpu.make_async_remote_copy(
            src_ref=out_ref.at[r, other, pl.ds(0, caps[r])],
            dst_ref=held[r][PLANES - off].at[pl.ds(0, caps[r])],
            send_sem=send_far.at[r, off],
            recv_sem=far_sem.at[r, PLANES - off],
            device_id=(to // nt, to % nt),
            device_id_type=MESH,
        )

    def own_copy(r):
        return pltpu.make_async_copy(
            out_ref.at[r, plane, pl.ds(0, caps[r])],
            held[r][0].at[pl.ds(0, caps[r])],
            far_sem.at[r, 0],
        )

    def near_copy(r, off, i):
        to = plane * members + (place + i) % members
        return pltpu.make_async_remote_copy(
            src_ref=packed.at[r, off, i],
            dst_ref=arr.at[r, off, (members - i) % members],
            send_sem=send_near.at[r, off, i],
            recv_sem=near_sem.at[r, off, (members - i) % members],
            device_id=(to // nt, to % nt),
            device_id_type=MESH,
        )

    def self_copy(r, off):
        return pltpu.make_async_copy(packed.at[r, off, 0], arr.at[r, off, 0], near_sem.at[r, off, 0])

    rounds = range(len(caps))
    for r in rounds:
        own_copy(r).start()
    for r in rounds:
        for off in FAR_ORDER:
            far_copy(r, off).start()

    def relay(r, off):
        for i in range(members):
            first = start_ref[((r * PLANES + off) * members) + i]
            packed[r, off, i] = held[r][off][pl.ds(first, each)]
            if i:
                near_copy(r, off, i).start()
            else:
                self_copy(r, off).start()

    for r in rounds:
        own_copy(r).wait()
        relay(r, 0)
    for r in rounds:
        for off in FAR_ORDER:
            far_copy(r, PLANES - off).wait_recv()
            relay(r, off)
    for r in rounds:
        for off in range(PLANES):
            self_copy(r, off).wait()
            for i in range(1, members):
                near_copy(r, off, i).wait_send()
                near_copy(r, off, members - i).wait_recv()
    for r in rounds:
        for off in FAR_ORDER:
            far_copy(r, off).wait_send()


def route(caps, starts, outgoing):
    nb, nt = lax.axis_size("band"), lax.axis_size("tile")
    rounds, _, most, fields, blk = outgoing.shape
    members = nb * nt // PLANES
    each = most // members
    block = (fields, blk)
    return pl.pallas_call(
        functools.partial(route_kernel, caps, nb, nt),
        out_shape=jax.ShapeDtypeStruct((rounds, PLANES, members, each) + block, BF),
        in_specs=[pl.BlockSpec(memory_space=pltpu.SMEM), pl.BlockSpec(memory_space=pl.ANY)],
        out_specs=pl.BlockSpec(memory_space=pl.ANY),
        scratch_shapes=[pltpu.VMEM((c + each,) + block, BF) for c in caps for _ in range(PLANES)]
        + [
            pltpu.VMEM((rounds, PLANES, members, each) + block, BF),
            pltpu.SemaphoreType.DMA((rounds, PLANES)),
            pltpu.SemaphoreType.DMA((rounds, PLANES, members)),
            pltpu.SemaphoreType.DMA((rounds, PLANES)),
            pltpu.SemaphoreType.DMA((rounds, PLANES, members)),
        ],
        compiler_params=pltpu.CompilerParams(
            has_side_effects=True, vmem_limit_bytes=VMEM_LIMIT
        ),
        name="route_packed" if caps[0] < most else "route_full",
    )(starts, outgoing)


def collect_kernel(slot_ref, arr_ref, out_ref, acc_ref):
    i = pl.program_id(0)
    n = arr_ref.shape[0]

    @pl.when(i == 0)
    def _():
        acc_ref[...] = jnp.zeros_like(acc_ref)

    def body(j, _):
        slot = slot_ref[i * n + j]
        acc_ref[slot] = acc_ref[slot] + arr_ref[j].astype(F32)
        return 0

    lax.fori_loop(0, n, body, 0, unroll=4)

    @pl.when(i == pl.num_programs(0) - 1)
    def _():
        out_ref[...] = acc_ref[: out_ref.shape[0]].astype(BF)


def collect(slots, arrived, slots_dev):
    count, fields, blk = arrived.shape
    steps = 8
    return pl.pallas_call(
        collect_kernel,
        out_shape=jax.ShapeDtypeStruct((slots_dev, fields, blk), BF),
        grid_spec=pltpu.PrefetchScalarGridSpec(
            num_scalar_prefetch=1,
            grid=(steps,),
            in_specs=[pl.BlockSpec((count // steps, fields, blk), lambda i, p: (i, 0, 0))],
            out_specs=pl.BlockSpec((slots_dev, fields, blk), lambda i, p: (0, 0, 0)),
            scratch_shapes=[pltpu.VMEM((slots_dev + 1, fields, blk), F32)],
        ),
        compiler_params=pltpu.CompilerParams(vmem_limit_bytes=VMEM_LIMIT),
        name="collect",
    )(slots, arrived)


def conv_kernel(
    first, x_ref, top_ref, bot_ref, left_ref, right_ref, wa_ref, wb_ref, b_ref, out_ref, *scratch
):
    if first:
        ends_ref, ends = scratch[0], scratch[-1]
        scratch = scratch[1:]
    sl, win, side = scratch[0], scratch[1], scratch[2]
    rows = out_ref.shape[0] if first else out_ref.shape[2]
    cols = sl.shape[1]
    width = sl.shape[2] // 2
    chan = x_ref.shape[1]
    slots = win.shape[0]
    side[0] = left_ref[0, CH : CH + rows, :].astype(F32)
    side[1] = right_ref[0, CH : CH + rows, :].astype(F32)

    def put(slot, pair, parity, row32, lo, hi):
        win[slot, 8 : 8 + cols, :] = row32
        win[slot, 7:8, :] = lo
        win[slot, 8 + cols : 9 + cols, :] = hi
        before = win[slot, 7 : 7 + cols, :]
        after = win[slot, 9 : 9 + cols, :]
        base = parity * width
        if first:
            g = before + pltpu.roll(row32, chan, 1) + pltpu.roll(after, 2 * chan, 1)
            sl[pair, :, base : base + width] = g.astype(BF)
        else:
            sl[pair, :, base : base + cols] = before.astype(BF)
            sl[pair, :, base + cols : base + 2 * cols] = row32.astype(BF)
            sl[pair, :, base + 2 * cols : base + 3 * cols] = after.astype(BF)

    def row_at(r):
        if first:
            y = x_ref[r].astype(F32)
            y = jnp.concatenate([y, jnp.zeros((cols - chan, cols), F32)], axis=0)
            return y.T
        return x_ref[r].astype(F32)

    def halo_row(ref):
        full = ref[0].astype(F32)
        return full[CH : CH + cols], full[CH - 1 : CH], full[CH + cols : CH + cols + 1]

    def put_row(r, k):
        put(
            k % slots,
            r // 2 + k % 2 if isinstance(r, int) else (r - k % 2) // 2 + k % 2,
            1 - k % 2,
            row_at(r),
            side[0, pl.ds(r, 1), :],
            side[1, pl.ds(r, 1), :],
        )

    row, lo, hi = halo_row(top_ref)
    put(0, 0, 0, row, lo, hi)
    row, lo, hi = halo_row(bot_ref)
    put(1, rows // 2, 1, row, lo, hi)
    unroll = UNROLLED
    n = 2 * PAIRS

    def fill_loop(i, _):
        for k in range(slots):
            put_row(i * slots + k, k)
        return 0

    def dots(p0):
        a = sl[pl.ds(p0, PAIRS)].reshape(PAIRS * cols, 2 * width)
        b = sl[pl.ds(p0 + 1, PAIRS)].reshape(PAIRS * cols, 2 * width)
        return jnp.dot(a, wa_ref[...], preferred_element_type=F32) + jnp.dot(
            b, wb_ref[...], preferred_element_type=F32
        )

    def finish(g, y):
        p0 = g * PAIRS
        hid = y.shape[1] // 2
        if first:
            y = gelu(y + b_ref[...])
            for p in range(PAIRS):
                for q in range(2):
                    part = y[p * cols : (p + 1) * cols, q * hid : (q + 1) * hid].astype(BF)
                    r = 2 * (p0 + p) + q
                    out_ref[r] = part
                    ends[0, pl.ds(r, 1), :] = part[:1].astype(F32)
                    ends[1, pl.ds(r, 1), :] = part[cols - 1 :].astype(F32)
            return
        flip = scratch[3].at[g % 2 if unroll else 0]
        for p in range(PAIRS):
            for q in range(2):
                part = y[p * cols : (p + 1) * cols, q * hid : (q + 1) * hid]
                flip[pl.ds(2 * p + q, hid, stride=n), :] = part.T

        def group(o, _):
            for j in range(8):
                v = flip[pl.ds((o * 8 + j) * n, n), :]
                out_ref[o * 8 + j, 0, pl.ds(g * n, n), :] = gelu(v + b_ref[o * 8 + j]).astype(BF)
            return 0

        if unroll:
            for o in range(hid // 8):
                group(o, 0)
        else:
            lax.fori_loop(0, hid // 8, group, 0)

    if unroll:
        for k in range(min(n + 2, rows)):
            put_row(k, k)
        for g in range(rows // n):
            y = dots(g * PAIRS)
            for k in range((g + 1) * n + 2, min((g + 2) * n + 2, rows)):
                put_row(k, k)
            finish(g, y)
    else:
        lax.fori_loop(0, rows // slots, fill_loop, 0)

        def chunk(g, _):
            finish(g, dots(g * PAIRS))
            return 0

        lax.fori_loop(0, rows // n, chunk, 0)
    if first:
        ends_ref[:, 0] = ends[...].astype(BF)


def conv(first, x, halos, weight, bias, face_count, rows, out_cols):
    top, bot, left, right = halos
    hid, chan = weight.shape[1], weight.shape[2]
    cols = out_cols
    w = weight.reshape(3, 3, hid, chan).transpose(0, 1, 3, 2)
    if first:
        w = w.reshape(3, 3 * chan, hid)
        w = jnp.pad(w, ((0, 0), (0, cols - 3 * chan), (0, 0)))
    else:
        w = w.reshape(3, 3 * chan, hid)
    width = w.shape[1]
    zero = jnp.zeros((width, hid), w.dtype)
    wide = [
        jnp.concatenate([w[a] if a < 3 else zero, w[a - 1] if a > 0 else zero], axis=1)
        for a in range(4)
    ]
    wa = jnp.concatenate(wide[:2], axis=0)
    wb = jnp.concatenate(wide[2:], axis=0)
    scratch = [
        pltpu.VMEM((rows // 2 + 1, cols, 2 * width), BF),
        pltpu.VMEM((8, cols + 16, cols), F32),
        pltpu.VMEM((2, rows, cols), F32),
    ]
    if first:
        bias_in = jnp.concatenate([bias, bias])[None, :]
        bias_spec = pl.BlockSpec((1, 2 * hid), lambda f: (0, 0))
        out_shape = (
            jax.ShapeDtypeStruct((face_count * rows, cols, hid), BF),
            jax.ShapeDtypeStruct((2, face_count, rows, hid), BF),
        )
        out_spec = (
            pl.BlockSpec((rows, cols, hid), lambda f: (f, 0, 0)),
            pl.BlockSpec((2, 1, rows, hid), lambda f: (0, f, 0, 0)),
        )
        scratch.append(pltpu.VMEM((2, rows, hid), F32))
    else:
        bias_in = bias
        bias_spec = pl.BlockSpec(memory_space=pltpu.SMEM)
        out_shape = jax.ShapeDtypeStruct((hid, face_count, rows, cols), BF)
        out_spec = pl.BlockSpec((hid, 1, rows, cols), lambda f: (0, f, 0, 0))
        scratch.append(pltpu.VMEM((2, hid * 2 * PAIRS, cols), F32))
    return pl.pallas_call(
        functools.partial(conv_kernel, first),
        out_shape=out_shape,
        grid=(face_count,),
        in_specs=[
            pl.BlockSpec((rows,) + x.shape[1:], lambda f: (f, 0, 0)),
            pl.BlockSpec((1,) + top.shape[1:], lambda f: (f, 0, 0)),
            pl.BlockSpec((1,) + bot.shape[1:], lambda f: (f, 0, 0)),
            pl.BlockSpec((1,) + left.shape[1:], lambda f: (f, 0, 0)),
            pl.BlockSpec((1,) + right.shape[1:], lambda f: (f, 0, 0)),
            pl.BlockSpec(wa.shape, lambda f: (0, 0)),
            pl.BlockSpec(wb.shape, lambda f: (0, 0)),
            bias_spec,
        ],
        out_specs=out_spec,
        scratch_shapes=scratch,
        compiler_params=pltpu.CompilerParams(vmem_limit_bytes=VMEM_LIMIT),
        name="conv1" if first else "conv2",
    )(x, top, bot, left, right, wa, wb, bias_in)


def halo_kernel(line_refs, nb, nt, tab_ref, *refs):
    ins, refs = refs[:line_refs], refs[line_refs:]
    tops, bots, lefts, rights, cand, pick, recv, send, met = refs
    faces, rows, cols = tops.shape[0], lefts.shape[1] - 2 * CH, tops.shape[1] - 2 * CH
    if line_refs == 2:
        top, bot = ins[0].at[:, 0], ins[0].at[:, rows - 1]
        left, right = ins[1].at[0], ins[1].at[1]
    else:
        top, bot, left, right = ins
    b, t = lax.axis_index("band"), lax.axis_index("tile")
    me = b * nt + t
    per_col, per_row = rows // CH, cols // CH
    chunks = nt * per_row
    classes = chunks // 2
    step = nb * nt // classes
    both = jnp.logical_and
    last_b, last_t = b == nb - 1, t == nt - 1
    TOP, BOT, LEFT, RIGHT = 0, 3, 6, 9
    main, lead = pl.ds(CH, cols), pl.ds(0, CH)
    main_v, trail_v = pl.ds(CH, rows), pl.ds(CH + rows, CH)
    trail = pl.ds(CH + cols, CH)
    started = []

    def go(cond, src, dst, sem, db, dt, own=True):
        same = db * nt + dt == me
        copy = pltpu.make_async_remote_copy(
            src_ref=src, dst_ref=dst, send_sem=send.at[len(started)], recv_sem=sem,
            device_id=(db, dt), device_id_type=MESH,
        )
        away = both(cond, jnp.logical_not(same)) if own else cond
        pl.when(away)(copy.start)
        if own:
            pl.when(both(cond, same))(pltpu.make_async_copy(src, dst, sem).start)
        started.append((away, copy))

    def taken(cond, ref, sem):
        pl.when(cond)(pltpu.make_async_copy(ref, ref, sem).wait)

    lines = [
        (b == 0, top, t * per_row, per_row),
        (last_b, bot, t * per_row, per_row),
        (t == 0, left, b * per_col, per_col),
        (last_t, right, b * per_col, per_col),
    ]
    for side, (cond, line, first, count) in enumerate(lines):
        for i in range(count):
            k = first + i
            upper = k // classes
            at = (k + upper * (chunks - 1 - 2 * k)) * step
            go(cond, line.at[:, pl.ds(i * CH, CH)], cand.at[upper, side], met, at // nt, at % nt)
    for cond, line, dst, base, db in (
        (b > 0, top, bots, BOT, b - 1),
        (b < nb - 1, bot, tops, TOP, b + 1),
    ):
        go(cond, line, dst.at[:, main], recv.at[base], db, t, False)
        go(both(cond, t > 0), line.at[:, pl.ds(0, CH)], dst.at[:, trail], recv.at[base + 2],
           db, t - 1, False)
        go(both(cond, t < nt - 1), line.at[:, pl.ds(cols - CH, CH)], dst.at[:, lead],
           recv.at[base + 1], db, t + 1, False)
    go(t > 0, left, rights.at[:, main_v], recv.at[RIGHT], b, t - 1, False)
    go(t < nt - 1, right, lefts.at[:, main_v], recv.at[LEFT], b, t + 1, False)

    meets = both(me % step == 0, me // step < classes)
    taken(meets, cand, met)
    near = lax.broadcasted_iota(jnp.int32, (CH, CH), 0)
    far = lax.broadcasted_iota(jnp.int32, (CH, CH), 1)
    mirror = jnp.where(near + far == CH - 1, 1.0, 0.0).astype(BF)

    @pl.when(meets)
    def _():
        def choose(f, _):
            for side in range(4):
                e = (f * 4 + side) * 3
                face, edge, rev = tab_ref[e], tab_ref[e + 1], tab_ref[e + 2]
                for h in range(2):
                    turned = jnp.dot(mirror, cand[1 - h, edge, face], preferred_element_type=F32)
                    pick[h, side, f] = jnp.where(
                        rev == 1, turned, cand[h, edge, face].astype(F32)
                    ).astype(BF)
            return 0

        lax.fori_loop(0, faces, choose, 0)

    low = me // step
    for h in range(2):
        k = low if h == 0 else chunks - 1 - low
        for side in range(4):
            src = pick.at[h, side]
            if side < 2:
                owner, off = k // per_row, k % per_row
                dst, base, db = ((tops, TOP, 0), (bots, BOT, nb - 1))[side]
                size, per, ends, length = nt, per_row, (lead, trail), cols
                dev = lambda o: (db, o)
            else:
                owner, off = k // per_col, k % per_col
                dst, base, dt = ((lefts, LEFT, 0), (rights, RIGHT, nt - 1))[side - 2]
                size, per, ends, length = nb, per_col, (lead, trail_v), rows
                dev = lambda o: (o, dt)
            go(meets, src, dst.at[:, pl.ds(CH + off * CH, CH)], recv.at[base], *dev(owner))
            go(both(meets, both(off == per - 1, owner < size - 1)), src, dst.at[:, ends[0]],
               recv.at[base + 1], *dev(owner + 1))
            go(both(meets, both(off == 0, owner > 0)), src, dst.at[:, ends[1]],
               recv.at[base + 2], *dev(owner - 1))

    for dst, base in ((tops, TOP), (bots, BOT)):
        taken(me >= 0, dst.at[:, main], recv.at[base])
        taken(t > 0, dst.at[:, lead], recv.at[base + 1])
        taken(t < nt - 1, dst.at[:, trail], recv.at[base + 2])
    for dst, base, cond in ((lefts, LEFT, t == 0), (rights, RIGHT, last_t)):
        taken(me >= 0, dst.at[:, main_v], recv.at[base])
        taken(both(cond, b > 0), dst.at[:, lead], recv.at[base + 1])
        taken(both(cond, b < nb - 1), dst.at[:, trail_v], recv.at[base + 2])

    for cond, src, end in ((t == 0, lefts, lead), (last_t, rights, trail)):
        for present, dst, part, row in (
            (b > 0, tops, lead, CH - 1),
            (b < nb - 1, bots, trail_v, 0),
        ):
            turn = ((CH - 1 if end is lead else 0) - row) % CH

            @pl.when(both(cond, present))
            def _():
                def corner(f, _):
                    v = src[f, part, :].astype(F32)
                    dst[f, end, :] = (pltpu.roll(v, turn, 0) if turn else v).astype(BF)
                    return 0

                lax.fori_loop(0, faces, corner, 0)

            @pl.when(both(cond, jnp.logical_not(present)))
            def _():
                dst[:, end, :] = jnp.zeros((faces, CH, dst.shape[2]), BF)

    for away, copy in started:
        pl.when(away)(copy.wait_send)


def halo_exchange(lines, seam_table, rows, cols, name):
    nb, nt = lax.axis_size("band"), lax.axis_size("tile")
    faces, chan = seam_table.shape[0], lines[0].shape[-1]
    per_col, per_row = rows // CH, cols // CH
    sends = 2 * per_col + 2 * per_row + 8 + 24
    row_line = jax.ShapeDtypeStruct((faces, cols + 2 * CH, chan), BF)
    col_line = jax.ShapeDtypeStruct((faces, rows + 2 * CH, chan), BF)
    vmem = pl.BlockSpec(memory_space=pltpu.VMEM)
    return pl.pallas_call(
        functools.partial(halo_kernel, len(lines), nb, nt),
        out_shape=(row_line, row_line, col_line, col_line),
        in_specs=[pl.BlockSpec(memory_space=pltpu.SMEM)]
        + [pl.BlockSpec(memory_space=pl.ANY)] * len(lines),
        out_specs=(vmem,) * 4,
        scratch_shapes=[
            pltpu.VMEM((2, 4, faces, CH, chan), BF),
            pltpu.VMEM((2, 4, faces, CH, chan), BF),
            pltpu.SemaphoreType.DMA((12,)),
            pltpu.SemaphoreType.DMA((sends,)),
            pltpu.SemaphoreType.DMA,
        ],
        compiler_params=pltpu.CompilerParams(has_side_effects=True),
        name=name,
    )(seam_table.reshape(-1), *lines)


def local(
    source,
    regrid_weights,
    dest_group,
    dest_block,
    seam_table,
    conv1_weight,
    conv1_bias,
    conv2_weight,
    conv2_bias,
):
    fields = source.shape[0]
    src_count, top_count, block_len, _ = regrid_weights.shape
    nb, nt = lax.axis_size("band"), lax.axis_size("tile")
    devices = nb * nt
    capacity = 3 * src_count * top_count // devices
    rows = block_len * nt // nb
    faces = seam_table.shape[0]
    slots_dev = faces * rows
    items = src_count * top_count
    target_dev = dest_group.reshape(items)
    target_slot = dest_block.reshape(items)
    onehot = (target_dev[:, None] == jnp.arange(devices, dtype=jnp.int32)[None, :]).astype(F32)
    earlier = (jnp.arange(items)[:, None] > jnp.arange(items)[None, :]).astype(BF)
    before = jnp.dot(earlier, onehot.astype(BF), preferred_element_type=F32)
    rank_in = jnp.sum(before * onehot, axis=1).astype(jnp.int32)
    each = capacity // ROUNDS
    members = devices // PLANES
    most = members * each
    slot_at = target_dev * capacity + rank_in
    hit = slot_at[None, :] == jnp.arange(devices * capacity, dtype=jnp.int32)[:, None]
    out_slots = slots_dev + jnp.sum(jnp.where(hit, target_slot[None, :] - slots_dev, 0), axis=1)

    def parts_of(count):
        r = jnp.arange(ROUNDS, dtype=jnp.int32).reshape((ROUNDS,) + (1,) * count.ndim)
        part = jnp.clip(count[None] - r * each, 0, each)
        part = part.reshape(part.shape[:-1] + (PLANES, members))
        lower = jnp.arange(members)[:, None] < jnp.arange(members)[None, :]
        before = jnp.sum(jnp.where(lower, part[..., :, None], 0), axis=-2)
        return before, jnp.sum(part, axis=-1)

    counts = jnp.sum(onehot, axis=0).astype(jnp.int32)
    first = parts_of(counts)[0].reshape(ROUNDS * devices)
    turn = rank_in // each
    mine = (turn * devices + target_dev)[:, None] == jnp.arange(ROUNDS * devices)[None, :]
    at = jnp.sum(jnp.where(mine, first[None, :], 0), axis=1)
    position = (turn * PLANES + target_dev // members) * most + at + rank_in % each
    outgoing = partials(position, source, regrid_weights, ROUNDS * PLANES * most)
    axes = ("band", "tile")
    told = jnp.concatenate(
        [out_slots.reshape(devices, capacity), jnp.broadcast_to(counts, (devices, devices))], axis=1
    )
    told = lax.all_to_all(told, axes, 0, 0, tiled=True)
    me = lax.axis_index("band") * nt + lax.axis_index("tile")
    plane, place = me // members, me % members
    starts, loads = parts_of(told[:, capacity:])
    starts = starts.reshape(ROUNDS, PLANES, members, PLANES, members)
    starts = lax.dynamic_slice(
        starts, (0, 0, place, plane, 0), (ROUNDS, PLANES, 1, 1, members)
    ).reshape(ROUNDS, PLANES, members)
    near = (plane + jnp.arange(PLANES, dtype=jnp.int32)) % PLANES
    there = (place + jnp.arange(members, dtype=jnp.int32)) % members
    from_there = (place + jnp.arange(members, dtype=jnp.int32)) % members
    starts = jnp.take(jnp.take(starts, near, axis=1), there, axis=2)
    arrived_slots = told[:, :capacity].reshape(PLANES, members, ROUNDS, each)
    arrived_slots = jnp.take(jnp.take(arrived_slots, near, axis=0), from_there, axis=1)
    arrived_slots = arrived_slots.transpose(2, 0, 1, 3)
    caps = (most * 5 // 6, most // 3)
    fits = jnp.all(jnp.max(loads, axis=(1, 2)) <= jnp.array(caps, dtype=jnp.int32))
    arrived = lax.cond(
        fits,
        functools.partial(route, caps),
        functools.partial(route, (most,) * ROUNDS),
        starts.reshape(-1),
        outgoing.reshape(ROUNDS, PLANES, most, fields, block_len),
    )
    grid = collect(
        arrived_slots.reshape(-1), arrived.reshape(devices * capacity, fields, block_len), slots_dev
    )
    tiles = grid.reshape(faces, rows, fields, block_len)
    pick = jnp.eye(block_len, dtype=BF)[jnp.array([0, block_len - 1])]
    ends = jnp.einsum("ep,tcp->etc", pick, grid, preferred_element_type=F32).astype(BF)
    ends = ends.reshape(2, faces, rows, fields)
    spare = ((0, 0), (0, 0), (0, block_len - fields))
    lines = [
        jnp.pad(tiles[:, 0].transpose(0, 2, 1), spare),
        jnp.pad(tiles[:, -1].transpose(0, 2, 1), spare),
        jnp.pad(ends[0], spare),
        jnp.pad(ends[1], spare),
    ]
    halos = halo_exchange(lines, seam_table, rows, block_len, "halo1")
    hidden, ends = conv(True, grid, halos, conv1_weight, conv1_bias, faces, rows, block_len)
    tiles = hidden.reshape(faces, rows, block_len, hidden.shape[2])
    halos = halo_exchange([tiles, ends], seam_table, rows, block_len, "halo2")
    return conv(False, hidden, halos, conv2_weight, conv2_bias, faces, rows, block_len)


def solution(mesh):
    return jax.shard_map(
        local,
        mesh=mesh,
        in_specs=(
            P(None, ("band", "tile")),
            P(("band", "tile"), None, None, None),
            P(("band", "tile"), None),
            P(("band", "tile"), None),
            P(),
            P(),
            P(),
            P(),
            P(),
        ),
        out_specs=P(None, None, "band", "tile"),
        check_vma=False,
    )
```

```python
import functools

import jax
import jax.numpy as jnp
from jax import lax
from jax.experimental import pallas as pl
from jax.experimental.pallas import tpu as pltpu
from jax.sharding import PartitionSpec as P

BF = jnp.bfloat16
F32 = jnp.float32
VMEM_LIMIT = 60 * 1024 * 1024
PAIRS = 8
PIECES = 2
CH = 16
PLANES = 4
ROUNDS = 2
FAR_ORDER = (2, 1, 3)
MESH = pl.DeviceIdType.MESH
GELU_COEF = (
    0.7978842684146765,
    0.03633414911622174,
    -3.30267008968913e-05,
    -5.527338755532785e-05,
    3.974071022505988e-06,
    -1.3378322650770525e-07,
    1.8139281733930472e-09,
)
GELU_CAP = 30.0


def gelu_of_half(h):
    u = jnp.minimum(h * h, 0.25 * GELU_CAP)
    coefs = [2.0 * 4.0**i * c for i, c in enumerate(GELU_COEF)]
    q = coefs[-1] * u + coefs[-2]
    for c in coefs[-3::-1]:
        q = q * u + c
    return h + h * jnp.tanh(h * q)


def partial_kernel(pos_ref, src_ref, w_ref, out_ref):
    s = pl.program_id(0)
    per_step = w_ref.shape[0]
    top, blk = w_ref.shape[1], w_ref.shape[2]

    @pl.when(s == 0)
    def _():
        out_ref[...] = jnp.zeros_like(out_ref)

    for j in range(per_step):
        x = src_ref[:, j * blk : (j + 1) * blk]
        for k in range(top):
            y = jnp.dot(x, w_ref[j, k], preferred_element_type=F32).astype(BF)
            out_ref[pos_ref[(s * per_step + j) * top + k]] = y


def partials(position, source, weights, slots):
    fields = source.shape[0]
    src_count, top, blk, _ = weights.shape
    step = min(16, src_count)
    return pl.pallas_call(
        partial_kernel,
        out_shape=jax.ShapeDtypeStruct((slots, fields, blk), BF),
        grid_spec=pltpu.PrefetchScalarGridSpec(
            num_scalar_prefetch=1,
            grid=(src_count // step,),
            in_specs=[
                pl.BlockSpec((fields, step * blk), lambda i, p: (0, i)),
                pl.BlockSpec((step, top, blk, blk), lambda i, p: (i, 0, 0, 0)),
            ],
            out_specs=pl.BlockSpec((slots, fields, blk), lambda i, p: (0, 0, 0)),
        ),
        compiler_params=pltpu.CompilerParams(vmem_limit_bytes=VMEM_LIMIT),
        name="partials",
    )(position, source, weights)


def route_kernel(caps, nb, nt, start_ref, out_ref, arr, *scratch):
    kept = len(caps) * PLANES
    packed, far_sem, near_sem, send_far, send_near = scratch[kept:]
    held = [scratch[r * PLANES : (r + 1) * PLANES] for r in range(len(caps))]
    members, each = packed.shape[2], packed.shape[3]
    me = lax.axis_index("band") * nt + lax.axis_index("tile")
    plane, place = me // members, me % members

    def far_copy(r, off):
        other = (plane + off) % PLANES
        to = other * members + place
        return pltpu.make_async_remote_copy(
            src_ref=out_ref.at[r, other, pl.ds(0, caps[r])],
            dst_ref=held[r][PLANES - off].at[pl.ds(0, caps[r])],
            send_sem=send_far.at[r, off],
            recv_sem=far_sem.at[r, PLANES - off],
            device_id=(to // nt, to % nt),
            device_id_type=MESH,
        )

    def own_copy(r):
        return pltpu.make_async_copy(
            out_ref.at[r, plane, pl.ds(0, caps[r])],
            held[r][0].at[pl.ds(0, caps[r])],
            far_sem.at[r, 0],
        )

    def near_copy(r, off, i):
        to = plane * members + (place + i) % members
        return pltpu.make_async_remote_copy(
            src_ref=packed.at[r, off, i],
            dst_ref=arr.at[r, off, (members - i) % members],
            send_sem=send_near.at[r, off, i],
            recv_sem=near_sem.at[r, off, (members - i) % members],
            device_id=(to // nt, to % nt),
            device_id_type=MESH,
        )

    def self_copy(r, off):
        return pltpu.make_async_copy(packed.at[r, off, 0], arr.at[r, off, 0], near_sem.at[r, off, 0])

    rounds = range(len(caps))
    for r in rounds:
        own_copy(r).start()
    for r in rounds:
        for off in FAR_ORDER:
            far_copy(r, off).start()

    def relay(r, off):
        for i in range(members):
            first = start_ref[((r * PLANES + off) * members) + i]
            packed[r, off, i] = held[r][off][pl.ds(first, each)]
            if i:
                near_copy(r, off, i).start()
            else:
                self_copy(r, off).start()

    for r in rounds:
        own_copy(r).wait()
        relay(r, 0)
    for r in rounds:
        for off in FAR_ORDER:
            far_copy(r, PLANES - off).wait_recv()
            relay(r, off)
    for r in rounds:
        for off in range(PLANES):
            self_copy(r, off).wait()
            for i in range(1, members):
                near_copy(r, off, i).wait_send()
                near_copy(r, off, members - i).wait_recv()
    for r in rounds:
        for off in FAR_ORDER:
            far_copy(r, off).wait_send()


def route(caps, starts, outgoing):
    nb, nt = lax.axis_size("band"), lax.axis_size("tile")
    rounds, _, most, fields, blk = outgoing.shape
    members = nb * nt // PLANES
    each = most // members
    block = (fields, blk)
    return pl.pallas_call(
        functools.partial(route_kernel, caps, nb, nt),
        out_shape=jax.ShapeDtypeStruct((rounds, PLANES, members, each) + block, BF),
        in_specs=[pl.BlockSpec(memory_space=pltpu.SMEM), pl.BlockSpec(memory_space=pl.ANY)],
        out_specs=pl.BlockSpec(memory_space=pl.ANY),
        scratch_shapes=[pltpu.VMEM((c + each,) + block, BF) for c in caps for _ in range(PLANES)]
        + [
            pltpu.VMEM((rounds, PLANES, members, each) + block, BF),
            pltpu.SemaphoreType.DMA((rounds, PLANES)),
            pltpu.SemaphoreType.DMA((rounds, PLANES, members)),
            pltpu.SemaphoreType.DMA((rounds, PLANES)),
            pltpu.SemaphoreType.DMA((rounds, PLANES, members)),
        ],
        compiler_params=pltpu.CompilerParams(
            has_side_effects=True, vmem_limit_bytes=VMEM_LIMIT
        ),
        name="route_packed" if caps[0] < most else "route_full",
    )(starts, outgoing)


def collect_kernel(slot_ref, arr_ref, out_ref, acc_ref):
    i = pl.program_id(0)
    n = arr_ref.shape[0]

    @pl.when(i == 0)
    def _():
        acc_ref[...] = jnp.zeros_like(acc_ref)

    def body(j, _):
        slot = slot_ref[i * n + j]
        acc_ref[slot] = acc_ref[slot] + arr_ref[j].astype(F32)
        return 0

    lax.fori_loop(0, n, body, 0, unroll=4)

    @pl.when(i == pl.num_programs(0) - 1)
    def _():
        out_ref[...] = acc_ref[: out_ref.shape[0]].astype(BF)


def collect(slots, arrived, slots_dev):
    count, fields, blk = arrived.shape
    steps = 8
    return pl.pallas_call(
        collect_kernel,
        out_shape=jax.ShapeDtypeStruct((slots_dev, fields, blk), BF),
        grid_spec=pltpu.PrefetchScalarGridSpec(
            num_scalar_prefetch=1,
            grid=(steps,),
            in_specs=[pl.BlockSpec((count // steps, fields, blk), lambda i, p: (i, 0, 0))],
            out_specs=pl.BlockSpec((slots_dev, fields, blk), lambda i, p: (0, 0, 0)),
            scratch_shapes=[pltpu.VMEM((slots_dev + 1, fields, blk), F32)],
        ),
        compiler_params=pltpu.CompilerParams(vmem_limit_bytes=VMEM_LIMIT),
        name="collect",
    )(slots, arrived)


def conv_kernel(
    first, x_ref, top_ref, bot_ref, left_ref, right_ref, w_ref, b_ref, out_ref, *scratch
):
    if first:
        ends_ref, ends = scratch[0], scratch[-1]
        scratch = scratch[1:]
    sl, win, side = scratch[0], scratch[1], scratch[2]
    rows = out_ref.shape[0] if first else out_ref.shape[2]
    cols = sl.shape[1]
    width = sl.shape[2] // 2
    chan = x_ref.shape[1]
    slots = win.shape[0]
    side[0] = left_ref[0, CH : CH + rows, :].astype(F32)
    side[1] = right_ref[0, CH : CH + rows, :].astype(F32)

    def put(slot, pair, parity, row32, lo, hi):
        win[slot, 8 : 8 + cols, :] = row32
        win[slot, 7:8, :] = lo
        win[slot, 8 + cols : 9 + cols, :] = hi
        before = win[slot, 7 : 7 + cols, :]
        after = win[slot, 9 : 9 + cols, :]
        base = parity * width
        if first:
            g = before + pltpu.roll(row32, chan, 1) + pltpu.roll(after, 2 * chan, 1)
            sl[pair, :, base : base + width] = g.astype(BF)
        else:
            sl[pair, :, base : base + cols] = before.astype(BF)
            sl[pair, :, base + cols : base + 2 * cols] = row32.astype(BF)
            sl[pair, :, base + 2 * cols : base + 3 * cols] = after.astype(BF)

    def row_at(r):
        if first:
            y = x_ref[r].astype(F32)
            y = jnp.concatenate([y, jnp.zeros((cols - chan, cols), F32)], axis=0)
            return y.T
        return x_ref[r].astype(F32)

    def halo_row(ref):
        full = ref[0].astype(F32)
        return full[CH : CH + cols], full[CH - 1 : CH], full[CH + cols : CH + cols + 1]

    def put_row(r, k):
        put(
            k % slots,
            r // 2 + k % 2 if isinstance(r, int) else (r - k % 2) // 2 + k % 2,
            1 - k % 2,
            row_at(r),
            side[0, pl.ds(r, 1), :],
            side[1, pl.ds(r, 1), :],
        )

    row, lo, hi = halo_row(top_ref)
    put(0, 0, 0, row, lo, hi)
    row, lo, hi = halo_row(bot_ref)
    put(1, rows // 2, 1, row, lo, hi)
    n = 2 * PAIRS
    chunks = rows // n
    hid = w_ref.shape[1] // 2
    held = scratch[3]

    per = PAIRS // PIECES

    def dots(g, piece):
        p0 = piece * per
        a = sl[pl.ds(g * PAIRS + p0, per)].reshape(per * cols, 2 * width)
        b = sl[pl.ds(g * PAIRS + p0 + 1, per)].reshape(per * cols, 2 * width)
        y = jnp.dot(
            jnp.concatenate([a, b], axis=1), w_ref[...], preferred_element_type=F32
        )
        if first:
            held[g % 2, p0 * cols : (p0 + per) * cols, :] = y
            return
        for p in range(per):
            for q in range(2):
                part = y[p * cols : (p + 1) * cols, q * hid : (q + 1) * hid]
                held[g % 2, pl.ds(2 * (p0 + p) + q, hid, stride=n), :] = part.T

    def finish(g, piece):
        slot = g % 2
        if first:
            for p in range(piece * per, (piece + 1) * per):
                y = gelu_of_half(held[slot, p * cols : (p + 1) * cols, :] + b_ref[...])
                for q in range(2):
                    part = y[:, q * hid : (q + 1) * hid].astype(BF)
                    r = 2 * (g * PAIRS + p) + q
                    out_ref[r] = part
                    ends[0, pl.ds(r, 1), :] = part[:1].astype(F32)
                    ends[1, pl.ds(r, 1), :] = part[cols - 1 :].astype(F32)
            return
        for o in range(hid * piece // PIECES, hid * (piece + 1) // PIECES):
            v = held[slot, o * n : (o + 1) * n, :]
            out_ref[o, 0, g * n : (g + 1) * n, :] = gelu_of_half(v + b_ref[o]).astype(BF)

    def put_for(g, piece):
        lo = g * n + 2 + piece * 2 * per if g or piece else 0
        for k in range(lo, min(g * n + 2 + (piece + 1) * 2 * per, rows)):
            put_row(k, k)

    for g in range(chunks + 1):
        for piece in range(PIECES):
            if g < chunks:
                put_for(g, piece)
                dots(g, piece)
            if g:
                finish(g - 1, piece)
    if first:
        ends_ref[:, 0] = ends[...].astype(BF)


def conv(first, x, halos, weight, bias, face_count, rows, out_cols):
    top, bot, left, right = halos
    hid, chan = weight.shape[1], weight.shape[2]
    cols = out_cols
    w = weight.reshape(3, 3, hid, chan).transpose(0, 1, 3, 2)
    if first:
        w = w.reshape(3, 3 * chan, hid)
        w = jnp.pad(w, ((0, 0), (0, cols - 3 * chan), (0, 0)))
    else:
        w = w.reshape(3, 3 * chan, hid)
    width = w.shape[1]
    zero = jnp.zeros((width, hid), w.dtype)
    wide = [
        jnp.concatenate([w[a] if a < 3 else zero, w[a - 1] if a > 0 else zero], axis=1)
        for a in range(4)
    ]
    w = jnp.concatenate(wide, axis=0) * 0.5
    bias = bias * 0.5
    scratch = [
        pltpu.VMEM((rows // 2 + 1, cols, 2 * width), BF),
        pltpu.VMEM((8, cols + 16, cols), F32),
        pltpu.VMEM((2, rows, cols), F32),
    ]
    if first:
        bias_in = jnp.concatenate([bias, bias])[None, :]
        bias_spec = pl.BlockSpec((1, 2 * hid), lambda f: (0, 0))
        out_shape = (
            jax.ShapeDtypeStruct((face_count * rows, cols, hid), BF),
            jax.ShapeDtypeStruct((2, face_count, rows, hid), BF),
        )
        out_spec = (
            pl.BlockSpec((rows, cols, hid), lambda f: (f, 0, 0)),
            pl.BlockSpec((2, 1, rows, hid), lambda f: (0, f, 0, 0)),
        )
        scratch.append(pltpu.VMEM((2, PAIRS * cols, 2 * hid), F32))
        scratch.append(pltpu.VMEM((2, rows, hid), F32))
    else:
        bias_in = bias
        bias_spec = pl.BlockSpec(memory_space=pltpu.SMEM)
        out_shape = jax.ShapeDtypeStruct((hid, face_count, rows, cols), BF)
        out_spec = pl.BlockSpec((hid, 1, rows, cols), lambda f: (0, f, 0, 0))
        scratch.append(pltpu.VMEM((2, hid * 2 * PAIRS, cols), F32))
    return pl.pallas_call(
        functools.partial(conv_kernel, first),
        out_shape=out_shape,
        grid=(face_count,),
        in_specs=[
            pl.BlockSpec((rows,) + x.shape[1:], lambda f: (f, 0, 0)),
            pl.BlockSpec((1,) + top.shape[1:], lambda f: (f, 0, 0)),
            pl.BlockSpec((1,) + bot.shape[1:], lambda f: (f, 0, 0)),
            pl.BlockSpec((1,) + left.shape[1:], lambda f: (f, 0, 0)),
            pl.BlockSpec((1,) + right.shape[1:], lambda f: (f, 0, 0)),
            pl.BlockSpec(w.shape, lambda f: (0, 0)),
            bias_spec,
        ],
        out_specs=out_spec,
        scratch_shapes=scratch,
        compiler_params=pltpu.CompilerParams(vmem_limit_bytes=VMEM_LIMIT),
        name="conv1" if first else "conv2",
    )(x, top, bot, left, right, w, bias_in)


def halo_kernel(line_refs, nb, nt, tab_ref, *refs):
    ins, refs = refs[:line_refs], refs[line_refs:]
    tops, bots, lefts, rights, cand, pick, recv, send, met = refs
    faces, rows, cols = tops.shape[0], lefts.shape[1] - 2 * CH, tops.shape[1] - 2 * CH
    if line_refs == 2:
        top, bot = ins[0].at[:, 0], ins[0].at[:, rows - 1]
        left, right = ins[1].at[0], ins[1].at[1]
    else:
        top, bot, left, right = ins
    b, t = lax.axis_index("band"), lax.axis_index("tile")
    me = b * nt + t
    per_col, per_row = rows // CH, cols // CH
    chunks = nt * per_row
    classes = chunks // 2
    step = nb * nt // classes
    both = jnp.logical_and
    last_b, last_t = b == nb - 1, t == nt - 1
    TOP, BOT, LEFT, RIGHT = 0, 3, 6, 9
    main, lead = pl.ds(CH, cols), pl.ds(0, CH)
    main_v, trail_v = pl.ds(CH, rows), pl.ds(CH + rows, CH)
    trail = pl.ds(CH + cols, CH)
    started = []

    def go(cond, src, dst, sem, db, dt, own=True):
        same = db * nt + dt == me
        copy = pltpu.make_async_remote_copy(
            src_ref=src, dst_ref=dst, send_sem=send.at[len(started)], recv_sem=sem,
            device_id=(db, dt), device_id_type=MESH,
        )
        away = both(cond, jnp.logical_not(same)) if own else cond
        pl.when(away)(copy.start)
        if own:
            pl.when(both(cond, same))(pltpu.make_async_copy(src, dst, sem).start)
        started.append((away, copy))

    def taken(cond, ref, sem):
        pl.when(cond)(pltpu.make_async_copy(ref, ref, sem).wait)

    lines = [
        (b == 0, top, t * per_row, per_row),
        (last_b, bot, t * per_row, per_row),
        (t == 0, left, b * per_col, per_col),
        (last_t, right, b * per_col, per_col),
    ]
    for side, (cond, line, first, count) in enumerate(lines):
        for i in range(count):
            k = first + i
            upper = k // classes
            at = (k + upper * (chunks - 1 - 2 * k)) * step
            go(cond, line.at[:, pl.ds(i * CH, CH)], cand.at[upper, side], met, at // nt, at % nt)
    for cond, line, dst, base, db in (
        (b > 0, top, bots, BOT, b - 1),
        (b < nb - 1, bot, tops, TOP, b + 1),
    ):
        go(cond, line, dst.at[:, main], recv.at[base], db, t, False)
        go(both(cond, t > 0), line.at[:, pl.ds(0, CH)], dst.at[:, trail], recv.at[base + 2],
           db, t - 1, False)
        go(both(cond, t < nt - 1), line.at[:, pl.ds(cols - CH, CH)], dst.at[:, lead],
           recv.at[base + 1], db, t + 1, False)
    go(t > 0, left, rights.at[:, main_v], recv.at[RIGHT], b, t - 1, False)
    go(t < nt - 1, right, lefts.at[:, main_v], recv.at[LEFT], b, t + 1, False)

    meets = both(me % step == 0, me // step < classes)
    taken(meets, cand, met)
    near = lax.broadcasted_iota(jnp.int32, (CH, CH), 0)
    far = lax.broadcasted_iota(jnp.int32, (CH, CH), 1)
    mirror = jnp.where(near + far == CH - 1, 1.0, 0.0).astype(BF)

    @pl.when(meets)
    def _():
        def choose(f, _):
            for side in range(4):
                e = (f * 4 + side) * 3
                face, edge, rev = tab_ref[e], tab_ref[e + 1], tab_ref[e + 2]
                for h in range(2):
                    turned = jnp.dot(mirror, cand[1 - h, edge, face], preferred_element_type=F32)
                    pick[h, side, f] = jnp.where(
                        rev == 1, turned, cand[h, edge, face].astype(F32)
                    ).astype(BF)
            return 0

        lax.fori_loop(0, faces, choose, 0)

    low = me // step
    for h in range(2):
        k = low if h == 0 else chunks - 1 - low
        for side in range(4):
            src = pick.at[h, side]
            if side < 2:
                owner, off = k // per_row, k % per_row
                dst, base, db = ((tops, TOP, 0), (bots, BOT, nb - 1))[side]
                size, per, ends, length = nt, per_row, (lead, trail), cols
                dev = lambda o: (db, o)
            else:
                owner, off = k // per_col, k % per_col
                dst, base, dt = ((lefts, LEFT, 0), (rights, RIGHT, nt - 1))[side - 2]
                size, per, ends, length = nb, per_col, (lead, trail_v), rows
                dev = lambda o: (o, dt)
            go(meets, src, dst.at[:, pl.ds(CH + off * CH, CH)], recv.at[base], *dev(owner))
            go(both(meets, both(off == per - 1, owner < size - 1)), src, dst.at[:, ends[0]],
               recv.at[base + 1], *dev(owner + 1))
            go(both(meets, both(off == 0, owner > 0)), src, dst.at[:, ends[1]],
               recv.at[base + 2], *dev(owner - 1))

    for dst, base in ((tops, TOP), (bots, BOT)):
        taken(me >= 0, dst.at[:, main], recv.at[base])
        taken(t > 0, dst.at[:, lead], recv.at[base + 1])
        taken(t < nt - 1, dst.at[:, trail], recv.at[base + 2])
    for dst, base, cond in ((lefts, LEFT, t == 0), (rights, RIGHT, last_t)):
        taken(me >= 0, dst.at[:, main_v], recv.at[base])
        taken(both(cond, b > 0), dst.at[:, lead], recv.at[base + 1])
        taken(both(cond, b < nb - 1), dst.at[:, trail_v], recv.at[base + 2])

    for cond, src, end in ((t == 0, lefts, lead), (last_t, rights, trail)):
        for present, dst, part, row in (
            (b > 0, tops, lead, CH - 1),
            (b < nb - 1, bots, trail_v, 0),
        ):
            turn = ((CH - 1 if end is lead else 0) - row) % CH

            @pl.when(both(cond, present))
            def _():
                def corner(f, _):
                    v = src[f, part, :].astype(F32)
                    dst[f, end, :] = (pltpu.roll(v, turn, 0) if turn else v).astype(BF)
                    return 0

                lax.fori_loop(0, faces, corner, 0)

            @pl.when(both(cond, jnp.logical_not(present)))
            def _():
                dst[:, end, :] = jnp.zeros((faces, CH, dst.shape[2]), BF)

    for away, copy in started:
        pl.when(away)(copy.wait_send)


def halo_exchange(lines, seam_table, rows, cols, name):
    nb, nt = lax.axis_size("band"), lax.axis_size("tile")
    faces, chan = seam_table.shape[0], lines[0].shape[-1]
    per_col, per_row = rows // CH, cols // CH
    sends = 2 * per_col + 2 * per_row + 8 + 24
    row_line = jax.ShapeDtypeStruct((faces, cols + 2 * CH, chan), BF)
    col_line = jax.ShapeDtypeStruct((faces, rows + 2 * CH, chan), BF)
    vmem = pl.BlockSpec(memory_space=pltpu.VMEM)
    return pl.pallas_call(
        functools.partial(halo_kernel, len(lines), nb, nt),
        out_shape=(row_line, row_line, col_line, col_line),
        in_specs=[pl.BlockSpec(memory_space=pltpu.SMEM)]
        + [pl.BlockSpec(memory_space=pl.ANY)] * len(lines),
        out_specs=(vmem,) * 4,
        scratch_shapes=[
            pltpu.VMEM((2, 4, faces, CH, chan), BF),
            pltpu.VMEM((2, 4, faces, CH, chan), BF),
            pltpu.SemaphoreType.DMA((12,)),
            pltpu.SemaphoreType.DMA((sends,)),
            pltpu.SemaphoreType.DMA,
        ],
        compiler_params=pltpu.CompilerParams(has_side_effects=True),
        name=name,
    )(seam_table.reshape(-1), *lines)


def local(
    source,
    regrid_weights,
    dest_group,
    dest_block,
    seam_table,
    conv1_weight,
    conv1_bias,
    conv2_weight,
    conv2_bias,
):
    fields = source.shape[0]
    src_count, top_count, block_len, _ = regrid_weights.shape
    nb, nt = lax.axis_size("band"), lax.axis_size("tile")
    devices = nb * nt
    capacity = 3 * src_count * top_count // devices
    rows = block_len * nt // nb
    faces = seam_table.shape[0]
    slots_dev = faces * rows
    items = src_count * top_count
    target_dev = dest_group.reshape(items)
    target_slot = dest_block.reshape(items)
    onehot = (target_dev[:, None] == jnp.arange(devices, dtype=jnp.int32)[None, :]).astype(F32)
    earlier = (jnp.arange(items)[:, None] > jnp.arange(items)[None, :]).astype(BF)
    before = jnp.dot(earlier, onehot.astype(BF), preferred_element_type=F32)
    rank_in = jnp.sum(before * onehot, axis=1).astype(jnp.int32)
    each = capacity // ROUNDS
    members = devices // PLANES
    most = members * each
    slot_at = target_dev * capacity + rank_in
    hit = slot_at[None, :] == jnp.arange(devices * capacity, dtype=jnp.int32)[:, None]
    out_slots = slots_dev + jnp.sum(jnp.where(hit, target_slot[None, :] - slots_dev, 0), axis=1)

    def parts_of(count):
        r = jnp.arange(ROUNDS, dtype=jnp.int32).reshape((ROUNDS,) + (1,) * count.ndim)
        part = jnp.clip(count[None] - r * each, 0, each)
        part = part.reshape(part.shape[:-1] + (PLANES, members))
        lower = jnp.arange(members)[:, None] < jnp.arange(members)[None, :]
        before = jnp.sum(jnp.where(lower, part[..., :, None], 0), axis=-2)
        return before, jnp.sum(part, axis=-1)

    counts = jnp.sum(onehot, axis=0).astype(jnp.int32)
    first = parts_of(counts)[0].reshape(ROUNDS * devices)
    turn = rank_in // each
    mine = (turn * devices + target_dev)[:, None] == jnp.arange(ROUNDS * devices)[None, :]
    at = jnp.sum(jnp.where(mine, first[None, :], 0), axis=1)
    position = (turn * PLANES + target_dev // members) * most + at + rank_in % each
    outgoing = partials(position, source, regrid_weights, ROUNDS * PLANES * most)
    axes = ("band", "tile")
    told = jnp.concatenate(
        [out_slots.reshape(devices, capacity), jnp.broadcast_to(counts, (devices, devices))], axis=1
    )
    told = lax.all_to_all(told, axes, 0, 0, tiled=True)
    me = lax.axis_index("band") * nt + lax.axis_index("tile")
    plane, place = me // members, me % members
    starts, loads = parts_of(told[:, capacity:])
    starts = starts.reshape(ROUNDS, PLANES, members, PLANES, members)
    starts = lax.dynamic_slice(
        starts, (0, 0, place, plane, 0), (ROUNDS, PLANES, 1, 1, members)
    ).reshape(ROUNDS, PLANES, members)
    near = (plane + jnp.arange(PLANES, dtype=jnp.int32)) % PLANES
    there = (place + jnp.arange(members, dtype=jnp.int32)) % members
    from_there = (place + jnp.arange(members, dtype=jnp.int32)) % members
    starts = jnp.take(jnp.take(starts, near, axis=1), there, axis=2)
    arrived_slots = told[:, :capacity].reshape(PLANES, members, ROUNDS, each)
    arrived_slots = jnp.take(jnp.take(arrived_slots, near, axis=0), from_there, axis=1)
    arrived_slots = arrived_slots.transpose(2, 0, 1, 3)
    caps = (most * 5 // 6, most // 3)
    fits = jnp.all(jnp.max(loads, axis=(1, 2)) <= jnp.array(caps, dtype=jnp.int32))
    arrived = lax.cond(
        fits,
        functools.partial(route, caps),
        functools.partial(route, (most,) * ROUNDS),
        starts.reshape(-1),
        outgoing.reshape(ROUNDS, PLANES, most, fields, block_len),
    )
    grid = collect(
        arrived_slots.reshape(-1), arrived.reshape(devices * capacity, fields, block_len), slots_dev
    )
    tiles = grid.reshape(faces, rows, fields, block_len)
    pick = jnp.eye(block_len, dtype=BF)[jnp.array([0, block_len - 1])]
    ends = jnp.einsum("ep,tcp->etc", pick, grid, preferred_element_type=F32).astype(BF)
    ends = ends.reshape(2, faces, rows, fields)
    spare = ((0, 0), (0, 0), (0, block_len - fields))
    lines = [
        jnp.pad(tiles[:, 0].transpose(0, 2, 1), spare),
        jnp.pad(tiles[:, -1].transpose(0, 2, 1), spare),
        jnp.pad(ends[0], spare),
        jnp.pad(ends[1], spare),
    ]
    halos = halo_exchange(lines, seam_table, rows, block_len, "halo1")
    hidden, ends = conv(True, grid, halos, conv1_weight, conv1_bias, faces, rows, block_len)
    tiles = hidden.reshape(faces, rows, block_len, hidden.shape[2])
    halos = halo_exchange([tiles, ends], seam_table, rows, block_len, "halo2")
    return conv(False, hidden, halos, conv2_weight, conv2_bias, faces, rows, block_len)


def solution(mesh):
    return jax.shard_map(
        local,
        mesh=mesh,
        in_specs=(
            P(None, ("band", "tile")),
            P(("band", "tile"), None, None, None),
            P(("band", "tile"), None),
            P(("band", "tile"), None),
            P(),
            P(),
            P(),
            P(),
            P(),
        ),
        out_specs=P(None, None, "band", "tile"),
        check_vma=False,
    )
```

```python
import functools

import jax
import jax.numpy as jnp
from jax import lax
from jax.experimental import pallas as pl
from jax.experimental.pallas import tpu as pltpu
from jax.sharding import PartitionSpec as P

BF = jnp.bfloat16
F32 = jnp.float32
VMEM_LIMIT = 60 * 1024 * 1024
PAIRS = 8
PIECES = 2
CH = 16
PLANES = 4
ROUNDS = 2
FAR_ORDER = (2, 1, 3)
MESH = pl.DeviceIdType.MESH
GELU_COEF = (
    0.7978842684146765,
    0.03633414911622174,
    -3.30267008968913e-05,
    -5.527338755532785e-05,
    3.974071022505988e-06,
    -1.3378322650770525e-07,
    1.8139281733930472e-09,
)
GELU_CAP = 30.0


def gelu_of_half(h):
    u = jnp.minimum(h * h, 0.25 * GELU_CAP)
    coefs = [2.0 * 4.0**i * c for i, c in enumerate(GELU_COEF)]
    q = coefs[-1] * u + coefs[-2]
    for c in coefs[-3::-1]:
        q = q * u + c
    return h + h * jnp.tanh(h * q)


def partial_kernel(pos_ref, src_ref, w_ref, out_ref):
    s = pl.program_id(0)
    per_step = w_ref.shape[0]
    top, blk = w_ref.shape[1], w_ref.shape[2]

    @pl.when(s == 0)
    def _():
        out_ref[...] = jnp.zeros_like(out_ref)

    for j in range(per_step):
        x = src_ref[:, j * blk : (j + 1) * blk]
        for k in range(top):
            y = jnp.dot(x, w_ref[j, k], preferred_element_type=F32).astype(BF)
            out_ref[pos_ref[(s * per_step + j) * top + k]] = y


def partials(position, source, weights, slots):
    fields = source.shape[0]
    src_count, top, blk, _ = weights.shape
    step = min(16, src_count)
    return pl.pallas_call(
        partial_kernel,
        out_shape=jax.ShapeDtypeStruct((slots, fields, blk), BF),
        grid_spec=pltpu.PrefetchScalarGridSpec(
            num_scalar_prefetch=1,
            grid=(src_count // step,),
            in_specs=[
                pl.BlockSpec((fields, step * blk), lambda i, p: (0, i)),
                pl.BlockSpec((step, top, blk, blk), lambda i, p: (i, 0, 0, 0)),
            ],
            out_specs=pl.BlockSpec((slots, fields, blk), lambda i, p: (0, 0, 0)),
        ),
        compiler_params=pltpu.CompilerParams(vmem_limit_bytes=VMEM_LIMIT),
        name="partials",
    )(position, source, weights)


def route_kernel(caps, nb, nt, start_ref, out_ref, arr, *scratch):
    kept = len(caps) * PLANES
    packed, far_sem, near_sem, send_far, send_near = scratch[kept:]
    held = [scratch[r * PLANES : (r + 1) * PLANES] for r in range(len(caps))]
    members, each = packed.shape[2], packed.shape[3]
    me = lax.axis_index("band") * nt + lax.axis_index("tile")
    plane, place = me // members, me % members

    def far_copy(r, off):
        other = (plane + off) % PLANES
        to = other * members + place
        return pltpu.make_async_remote_copy(
            src_ref=out_ref.at[r, other, pl.ds(0, caps[r])],
            dst_ref=held[r][PLANES - off].at[pl.ds(0, caps[r])],
            send_sem=send_far.at[r, off],
            recv_sem=far_sem.at[r, PLANES - off],
            device_id=(to // nt, to % nt),
            device_id_type=MESH,
        )

    def own_copy(r):
        return pltpu.make_async_copy(
            out_ref.at[r, plane, pl.ds(0, caps[r])],
            held[r][0].at[pl.ds(0, caps[r])],
            far_sem.at[r, 0],
        )

    def near_copy(r, off, i):
        to = plane * members + (place + i) % members
        return pltpu.make_async_remote_copy(
            src_ref=packed.at[r, off, i],
            dst_ref=arr.at[r, off, (members - i) % members],
            send_sem=send_near.at[r, off, i],
            recv_sem=near_sem.at[r, off, (members - i) % members],
            device_id=(to // nt, to % nt),
            device_id_type=MESH,
        )

    def self_copy(r, off):
        return pltpu.make_async_copy(packed.at[r, off, 0], arr.at[r, off, 0], near_sem.at[r, off, 0])

    rounds = range(len(caps))
    for r in rounds:
        own_copy(r).start()
    for r in rounds:
        for off in FAR_ORDER:
            far_copy(r, off).start()

    def relay(r, off):
        for i in range(members):
            first = start_ref[((r * PLANES + off) * members) + i]
            packed[r, off, i] = held[r][off][pl.ds(first, each)]
            if i:
                near_copy(r, off, i).start()
            else:
                self_copy(r, off).start()

    for r in rounds:
        own_copy(r).wait()
        relay(r, 0)
    for r in rounds:
        for off in FAR_ORDER:
            far_copy(r, PLANES - off).wait_recv()
            relay(r, off)
    for r in rounds:
        for off in range(PLANES):
            self_copy(r, off).wait()
            for i in range(1, members):
                near_copy(r, off, i).wait_send()
                near_copy(r, off, members - i).wait_recv()
    for r in rounds:
        for off in FAR_ORDER:
            far_copy(r, off).wait_send()


def route(caps, starts, outgoing):
    nb, nt = lax.axis_size("band"), lax.axis_size("tile")
    rounds, _, most, fields, blk = outgoing.shape
    members = nb * nt // PLANES
    each = most // members
    block = (fields, blk)
    return pl.pallas_call(
        functools.partial(route_kernel, caps, nb, nt),
        out_shape=jax.ShapeDtypeStruct((rounds, PLANES, members, each) + block, BF),
        in_specs=[pl.BlockSpec(memory_space=pltpu.SMEM), pl.BlockSpec(memory_space=pl.ANY)],
        out_specs=pl.BlockSpec(memory_space=pl.ANY),
        scratch_shapes=[pltpu.VMEM((c + each,) + block, BF) for c in caps for _ in range(PLANES)]
        + [
            pltpu.VMEM((rounds, PLANES, members, each) + block, BF),
            pltpu.SemaphoreType.DMA((rounds, PLANES)),
            pltpu.SemaphoreType.DMA((rounds, PLANES, members)),
            pltpu.SemaphoreType.DMA((rounds, PLANES)),
            pltpu.SemaphoreType.DMA((rounds, PLANES, members)),
        ],
        compiler_params=pltpu.CompilerParams(
            has_side_effects=True, vmem_limit_bytes=VMEM_LIMIT
        ),
        name="route_" + "_".join(map(str, caps)),
    )(starts, outgoing)


def collect_kernel(slot_ref, arr_ref, out_ref, acc_ref):
    i = pl.program_id(0)
    n = arr_ref.shape[0]

    @pl.when(i == 0)
    def _():
        acc_ref[...] = jnp.zeros_like(acc_ref)

    def body(j, _):
        slot = slot_ref[i * n + j]
        acc_ref[slot] = acc_ref[slot] + arr_ref[j].astype(F32)
        return 0

    lax.fori_loop(0, n, body, 0, unroll=4)

    @pl.when(i == pl.num_programs(0) - 1)
    def _():
        out_ref[...] = acc_ref[: out_ref.shape[0]].astype(BF)


def collect(slots, arrived, slots_dev):
    count, fields, blk = arrived.shape
    steps = 8
    return pl.pallas_call(
        collect_kernel,
        out_shape=jax.ShapeDtypeStruct((slots_dev, fields, blk), BF),
        grid_spec=pltpu.PrefetchScalarGridSpec(
            num_scalar_prefetch=1,
            grid=(steps,),
            in_specs=[pl.BlockSpec((count // steps, fields, blk), lambda i, p: (i, 0, 0))],
            out_specs=pl.BlockSpec((slots_dev, fields, blk), lambda i, p: (0, 0, 0)),
            scratch_shapes=[pltpu.VMEM((slots_dev + 1, fields, blk), F32)],
        ),
        compiler_params=pltpu.CompilerParams(vmem_limit_bytes=VMEM_LIMIT),
        name="collect",
    )(slots, arrived)


def conv_kernel(
    first, x_ref, top_ref, bot_ref, left_ref, right_ref, w_ref, b_ref, out_ref, *scratch
):
    if first:
        ends_ref, ends = scratch[0], scratch[-1]
        scratch = scratch[1:]
    sl, win, side = scratch[0], scratch[1], scratch[2]
    rows = out_ref.shape[0] if first else out_ref.shape[2]
    cols = sl.shape[1]
    width = sl.shape[2] // 2
    chan = x_ref.shape[1]
    slots = win.shape[0]
    side[0] = left_ref[0, CH : CH + rows, :].astype(F32)
    side[1] = right_ref[0, CH : CH + rows, :].astype(F32)

    def put(slot, pair, parity, row32, lo, hi):
        win[slot, 8 : 8 + cols, :] = row32
        win[slot, 7:8, :] = lo
        win[slot, 8 + cols : 9 + cols, :] = hi
        before = win[slot, 7 : 7 + cols, :]
        after = win[slot, 9 : 9 + cols, :]
        base = parity * width
        if first:
            g = before + pltpu.roll(row32, chan, 1) + pltpu.roll(after, 2 * chan, 1)
            sl[pair, :, base : base + width] = g.astype(BF)
        else:
            sl[pair, :, base : base + cols] = before.astype(BF)
            sl[pair, :, base + cols : base + 2 * cols] = row32.astype(BF)
            sl[pair, :, base + 2 * cols : base + 3 * cols] = after.astype(BF)

    def row_at(r):
        if first:
            y = x_ref[r].astype(F32)
            y = jnp.concatenate([y, jnp.zeros((cols - chan, cols), F32)], axis=0)
            return y.T
        return x_ref[r].astype(F32)

    def halo_row(ref):
        full = ref[0].astype(F32)
        return full[CH : CH + cols], full[CH - 1 : CH], full[CH + cols : CH + cols + 1]

    def put_row(r, k):
        put(
            k % slots,
            r // 2 + k % 2 if isinstance(r, int) else (r - k % 2) // 2 + k % 2,
            1 - k % 2,
            row_at(r),
            side[0, pl.ds(r, 1), :],
            side[1, pl.ds(r, 1), :],
        )

    row, lo, hi = halo_row(top_ref)
    put(0, 0, 0, row, lo, hi)
    row, lo, hi = halo_row(bot_ref)
    put(1, rows // 2, 1, row, lo, hi)
    n = 2 * PAIRS
    chunks = rows // n
    hid = w_ref.shape[1] // 2
    held = scratch[3]

    per = PAIRS // PIECES

    def dots(g, piece):
        p0 = piece * per
        a = sl[pl.ds(g * PAIRS + p0, per)].reshape(per * cols, 2 * width)
        b = sl[pl.ds(g * PAIRS + p0 + 1, per)].reshape(per * cols, 2 * width)
        y = jnp.dot(
            jnp.concatenate([a, b], axis=1), w_ref[...], preferred_element_type=F32
        )
        if first:
            held[g % 2, p0 * cols : (p0 + per) * cols, :] = y
            return
        for p in range(per):
            for q in range(2):
                part = y[p * cols : (p + 1) * cols, q * hid : (q + 1) * hid]
                held[g % 2, pl.ds(2 * (p0 + p) + q, hid, stride=n), :] = part.T

    def finish(g, piece):
        slot = g % 2
        if first:
            for p in range(piece * per, (piece + 1) * per):
                y = gelu_of_half(held[slot, p * cols : (p + 1) * cols, :] + b_ref[...])
                for q in range(2):
                    part = y[:, q * hid : (q + 1) * hid].astype(BF)
                    r = 2 * (g * PAIRS + p) + q
                    out_ref[r] = part
                    ends[0, pl.ds(r, 1), :] = part[:1].astype(F32)
                    ends[1, pl.ds(r, 1), :] = part[cols - 1 :].astype(F32)
            return
        for o in range(hid * piece // PIECES, hid * (piece + 1) // PIECES):
            v = held[slot, o * n : (o + 1) * n, :]
            out_ref[o, 0, g * n : (g + 1) * n, :] = gelu_of_half(v + b_ref[o]).astype(BF)

    def put_for(g, piece):
        lo = g * n + 2 + piece * 2 * per if g or piece else 0
        for k in range(lo, min(g * n + 2 + (piece + 1) * 2 * per, rows)):
            put_row(k, k)

    for g in range(chunks + 1):
        for piece in range(PIECES):
            if g < chunks:
                put_for(g, piece)
                dots(g, piece)
            if g:
                finish(g - 1, piece)
    if first:
        ends_ref[:, 0] = ends[...].astype(BF)


def conv(first, x, halos, weight, bias, face_count, rows, out_cols):
    top, bot, left, right = halos
    hid, chan = weight.shape[1], weight.shape[2]
    cols = out_cols
    w = weight.reshape(3, 3, hid, chan).transpose(0, 1, 3, 2)
    if first:
        w = w.reshape(3, 3 * chan, hid)
        w = jnp.pad(w, ((0, 0), (0, cols - 3 * chan), (0, 0)))
    else:
        w = w.reshape(3, 3 * chan, hid)
    width = w.shape[1]
    zero = jnp.zeros((width, hid), w.dtype)
    wide = [
        jnp.concatenate([w[a] if a < 3 else zero, w[a - 1] if a > 0 else zero], axis=1)
        for a in range(4)
    ]
    w = jnp.concatenate(wide, axis=0) * 0.5
    bias = bias * 0.5
    scratch = [
        pltpu.VMEM((rows // 2 + 1, cols, 2 * width), BF),
        pltpu.VMEM((8, cols + 16, cols), F32),
        pltpu.VMEM((2, rows, cols), F32),
    ]
    if first:
        bias_in = jnp.concatenate([bias, bias])[None, :]
        bias_spec = pl.BlockSpec((1, 2 * hid), lambda f: (0, 0))
        out_shape = (
            jax.ShapeDtypeStruct((face_count * rows, cols, hid), BF),
            jax.ShapeDtypeStruct((2, face_count, rows, hid), BF),
        )
        out_spec = (
            pl.BlockSpec((rows, cols, hid), lambda f: (f, 0, 0)),
            pl.BlockSpec((2, 1, rows, hid), lambda f: (0, f, 0, 0)),
        )
        scratch.append(pltpu.VMEM((2, PAIRS * cols, 2 * hid), F32))
        scratch.append(pltpu.VMEM((2, rows, hid), F32))
    else:
        bias_in = bias
        bias_spec = pl.BlockSpec(memory_space=pltpu.SMEM)
        out_shape = jax.ShapeDtypeStruct((hid, face_count, rows, cols), BF)
        out_spec = pl.BlockSpec((hid, 1, rows, cols), lambda f: (0, f, 0, 0))
        scratch.append(pltpu.VMEM((2, hid * 2 * PAIRS, cols), F32))
    return pl.pallas_call(
        functools.partial(conv_kernel, first),
        out_shape=out_shape,
        grid=(face_count,),
        in_specs=[
            pl.BlockSpec((rows,) + x.shape[1:], lambda f: (f, 0, 0)),
            pl.BlockSpec((1,) + top.shape[1:], lambda f: (f, 0, 0)),
            pl.BlockSpec((1,) + bot.shape[1:], lambda f: (f, 0, 0)),
            pl.BlockSpec((1,) + left.shape[1:], lambda f: (f, 0, 0)),
            pl.BlockSpec((1,) + right.shape[1:], lambda f: (f, 0, 0)),
            pl.BlockSpec(w.shape, lambda f: (0, 0)),
            bias_spec,
        ],
        out_specs=out_spec,
        scratch_shapes=scratch,
        compiler_params=pltpu.CompilerParams(vmem_limit_bytes=VMEM_LIMIT),
        name="conv1" if first else "conv2",
    )(x, top, bot, left, right, w, bias_in)


def halo_kernel(line_refs, nb, nt, tab_ref, *refs):
    ins, refs = refs[:line_refs], refs[line_refs:]
    tops, bots, lefts, rights, cand, pick, recv, send, met = refs
    faces, rows, cols = tops.shape[0], lefts.shape[1] - 2 * CH, tops.shape[1] - 2 * CH
    if line_refs == 2:
        top, bot = ins[0].at[:, 0], ins[0].at[:, rows - 1]
        left, right = ins[1].at[0], ins[1].at[1]
    else:
        top, bot, left, right = ins
    b, t = lax.axis_index("band"), lax.axis_index("tile")
    me = b * nt + t
    per_col, per_row = rows // CH, cols // CH
    chunks = nt * per_row
    classes = chunks // 2
    step = nb * nt // classes
    both = jnp.logical_and
    last_b, last_t = b == nb - 1, t == nt - 1
    TOP, BOT, LEFT, RIGHT = 0, 3, 6, 9
    main, lead = pl.ds(CH, cols), pl.ds(0, CH)
    main_v, trail_v = pl.ds(CH, rows), pl.ds(CH + rows, CH)
    trail = pl.ds(CH + cols, CH)
    started = []

    def go(cond, src, dst, sem, db, dt, own=True):
        same = db * nt + dt == me
        copy = pltpu.make_async_remote_copy(
            src_ref=src, dst_ref=dst, send_sem=send.at[len(started)], recv_sem=sem,
            device_id=(db, dt), device_id_type=MESH,
        )
        away = both(cond, jnp.logical_not(same)) if own else cond
        pl.when(away)(copy.start)
        if own:
            pl.when(both(cond, same))(pltpu.make_async_copy(src, dst, sem).start)
        started.append((away, copy))

    def taken(cond, ref, sem):
        pl.when(cond)(pltpu.make_async_copy(ref, ref, sem).wait)

    lines = [
        (b == 0, top, t * per_row, per_row),
        (last_b, bot, t * per_row, per_row),
        (t == 0, left, b * per_col, per_col),
        (last_t, right, b * per_col, per_col),
    ]
    for side, (cond, line, first, count) in enumerate(lines):
        for i in range(count):
            k = first + i
            upper = k // classes
            at = (k + upper * (chunks - 1 - 2 * k)) * step
            go(cond, line.at[:, pl.ds(i * CH, CH)], cand.at[upper, side], met, at // nt, at % nt)
    for cond, line, dst, base, db in (
        (b > 0, top, bots, BOT, b - 1),
        (b < nb - 1, bot, tops, TOP, b + 1),
    ):
        go(cond, line, dst.at[:, main], recv.at[base], db, t, False)
        go(both(cond, t > 0), line.at[:, pl.ds(0, CH)], dst.at[:, trail], recv.at[base + 2],
           db, t - 1, False)
        go(both(cond, t < nt - 1), line.at[:, pl.ds(cols - CH, CH)], dst.at[:, lead],
           recv.at[base + 1], db, t + 1, False)
    go(t > 0, left, rights.at[:, main_v], recv.at[RIGHT], b, t - 1, False)
    go(t < nt - 1, right, lefts.at[:, main_v], recv.at[LEFT], b, t + 1, False)

    meets = both(me % step == 0, me // step < classes)
    taken(meets, cand, met)
    near = lax.broadcasted_iota(jnp.int32, (CH, CH), 0)
    far = lax.broadcasted_iota(jnp.int32, (CH, CH), 1)
    mirror = jnp.where(near + far == CH - 1, 1.0, 0.0).astype(BF)

    @pl.when(meets)
    def _():
        def choose(f, _):
            for side in range(4):
                e = (f * 4 + side) * 3
                face, edge, rev = tab_ref[e], tab_ref[e + 1], tab_ref[e + 2]
                for h in range(2):
                    turned = jnp.dot(mirror, cand[1 - h, edge, face], preferred_element_type=F32)
                    pick[h, side, f] = jnp.where(
                        rev == 1, turned, cand[h, edge, face].astype(F32)
                    ).astype(BF)
            return 0

        lax.fori_loop(0, faces, choose, 0)

    low = me // step
    for h in range(2):
        k = low if h == 0 else chunks - 1 - low
        for side in range(4):
            src = pick.at[h, side]
            if side < 2:
                owner, off = k // per_row, k % per_row
                dst, base, db = ((tops, TOP, 0), (bots, BOT, nb - 1))[side]
                size, per, ends, length = nt, per_row, (lead, trail), cols
                dev = lambda o: (db, o)
            else:
                owner, off = k // per_col, k % per_col
                dst, base, dt = ((lefts, LEFT, 0), (rights, RIGHT, nt - 1))[side - 2]
                size, per, ends, length = nb, per_col, (lead, trail_v), rows
                dev = lambda o: (o, dt)
            go(meets, src, dst.at[:, pl.ds(CH + off * CH, CH)], recv.at[base], *dev(owner))
            go(both(meets, both(off == per - 1, owner < size - 1)), src, dst.at[:, ends[0]],
               recv.at[base + 1], *dev(owner + 1))
            go(both(meets, both(off == 0, owner > 0)), src, dst.at[:, ends[1]],
               recv.at[base + 2], *dev(owner - 1))

    for dst, base in ((tops, TOP), (bots, BOT)):
        taken(me >= 0, dst.at[:, main], recv.at[base])
        taken(t > 0, dst.at[:, lead], recv.at[base + 1])
        taken(t < nt - 1, dst.at[:, trail], recv.at[base + 2])
    for dst, base, cond in ((lefts, LEFT, t == 0), (rights, RIGHT, last_t)):
        taken(me >= 0, dst.at[:, main_v], recv.at[base])
        taken(both(cond, b > 0), dst.at[:, lead], recv.at[base + 1])
        taken(both(cond, b < nb - 1), dst.at[:, trail_v], recv.at[base + 2])

    for cond, src, end in ((t == 0, lefts, lead), (last_t, rights, trail)):
        for present, dst, part, row in (
            (b > 0, tops, lead, CH - 1),
            (b < nb - 1, bots, trail_v, 0),
        ):
            turn = ((CH - 1 if end is lead else 0) - row) % CH

            @pl.when(both(cond, present))
            def _():
                def corner(f, _):
                    v = src[f, part, :].astype(F32)
                    dst[f, end, :] = (pltpu.roll(v, turn, 0) if turn else v).astype(BF)
                    return 0

                lax.fori_loop(0, faces, corner, 0)

            @pl.when(both(cond, jnp.logical_not(present)))
            def _():
                dst[:, end, :] = jnp.zeros((faces, CH, dst.shape[2]), BF)

    for away, copy in started:
        pl.when(away)(copy.wait_send)


def halo_exchange(lines, seam_table, rows, cols, name):
    nb, nt = lax.axis_size("band"), lax.axis_size("tile")
    faces, chan = seam_table.shape[0], lines[0].shape[-1]
    per_col, per_row = rows // CH, cols // CH
    sends = 2 * per_col + 2 * per_row + 8 + 24
    row_line = jax.ShapeDtypeStruct((faces, cols + 2 * CH, chan), BF)
    col_line = jax.ShapeDtypeStruct((faces, rows + 2 * CH, chan), BF)
    vmem = pl.BlockSpec(memory_space=pltpu.VMEM)
    return pl.pallas_call(
        functools.partial(halo_kernel, len(lines), nb, nt),
        out_shape=(row_line, row_line, col_line, col_line),
        in_specs=[pl.BlockSpec(memory_space=pltpu.SMEM)]
        + [pl.BlockSpec(memory_space=pl.ANY)] * len(lines),
        out_specs=(vmem,) * 4,
        scratch_shapes=[
            pltpu.VMEM((2, 4, faces, CH, chan), BF),
            pltpu.VMEM((2, 4, faces, CH, chan), BF),
            pltpu.SemaphoreType.DMA((12,)),
            pltpu.SemaphoreType.DMA((sends,)),
            pltpu.SemaphoreType.DMA,
        ],
        compiler_params=pltpu.CompilerParams(has_side_effects=True),
        name=name,
    )(seam_table.reshape(-1), *lines)


def local(
    source,
    regrid_weights,
    dest_group,
    dest_block,
    seam_table,
    conv1_weight,
    conv1_bias,
    conv2_weight,
    conv2_bias,
):
    fields = source.shape[0]
    src_count, top_count, block_len, _ = regrid_weights.shape
    nb, nt = lax.axis_size("band"), lax.axis_size("tile")
    devices = nb * nt
    capacity = 3 * src_count * top_count // devices
    rows = block_len * nt // nb
    faces = seam_table.shape[0]
    slots_dev = faces * rows
    items = src_count * top_count
    target_dev = dest_group.reshape(items)
    target_slot = dest_block.reshape(items)
    onehot = (target_dev[:, None] == jnp.arange(devices, dtype=jnp.int32)[None, :]).astype(F32)
    earlier = (jnp.arange(items)[:, None] > jnp.arange(items)[None, :]).astype(BF)
    before = jnp.dot(earlier, onehot.astype(BF), preferred_element_type=F32)
    rank_in = jnp.sum(before * onehot, axis=1).astype(jnp.int32)
    each = capacity // ROUNDS
    members = devices // PLANES
    most = members * each
    slot_at = target_dev * capacity + rank_in
    hit = slot_at[None, :] == jnp.arange(devices * capacity, dtype=jnp.int32)[:, None]
    out_slots = slots_dev + jnp.sum(jnp.where(hit, target_slot[None, :] - slots_dev, 0), axis=1)

    def parts_of(count):
        r = jnp.arange(ROUNDS, dtype=jnp.int32).reshape((ROUNDS,) + (1,) * count.ndim)
        part = jnp.clip(count[None] - r * each, 0, each)
        part = part.reshape(part.shape[:-1] + (PLANES, members))
        lower = jnp.arange(members)[:, None] < jnp.arange(members)[None, :]
        before = jnp.sum(jnp.where(lower, part[..., :, None], 0), axis=-2)
        return before, jnp.sum(part, axis=-1)

    counts = jnp.sum(onehot, axis=0).astype(jnp.int32)
    first = parts_of(counts)[0].reshape(ROUNDS * devices)
    turn = rank_in // each
    mine = (turn * devices + target_dev)[:, None] == jnp.arange(ROUNDS * devices)[None, :]
    at = jnp.sum(jnp.where(mine, first[None, :], 0), axis=1)
    position = (turn * PLANES + target_dev // members) * most + at + rank_in % each
    outgoing = partials(position, source, regrid_weights, ROUNDS * PLANES * most)
    axes = ("band", "tile")
    told = jnp.concatenate(
        [out_slots.reshape(devices, capacity), jnp.broadcast_to(counts, (devices, devices))], axis=1
    )
    told = lax.all_to_all(told, axes, 0, 0, tiled=True)
    me = lax.axis_index("band") * nt + lax.axis_index("tile")
    plane, place = me // members, me % members
    starts, loads = parts_of(told[:, capacity:])
    starts = starts.reshape(ROUNDS, PLANES, members, PLANES, members)
    starts = lax.dynamic_slice(
        starts, (0, 0, place, plane, 0), (ROUNDS, PLANES, 1, 1, members)
    ).reshape(ROUNDS, PLANES, members)
    near = (plane + jnp.arange(PLANES, dtype=jnp.int32)) % PLANES
    there = (place + jnp.arange(members, dtype=jnp.int32)) % members
    from_there = (place + jnp.arange(members, dtype=jnp.int32)) % members
    starts = jnp.take(jnp.take(starts, near, axis=1), there, axis=2)
    arrived_slots = told[:, :capacity].reshape(PLANES, members, ROUNDS, each)
    arrived_slots = jnp.take(jnp.take(arrived_slots, near, axis=0), from_there, axis=1)
    arrived_slots = arrived_slots.transpose(2, 0, 1, 3)
    peak = jnp.max(loads, axis=(1, 2))
    levels = [(most * 5 // 6, most // 4), (most * 5 // 6, most // 3), (most,) * ROUNDS]
    fit = [jnp.all(peak <= jnp.array(caps, dtype=jnp.int32)) for caps in levels[:-1]]
    arrived = lax.switch(
        jnp.where(fit[0], 0, jnp.where(fit[1], 1, 2)),
        [functools.partial(route, caps) for caps in levels],
        starts.reshape(-1),
        outgoing.reshape(ROUNDS, PLANES, most, fields, block_len),
    )
    grid = collect(
        arrived_slots.reshape(-1), arrived.reshape(devices * capacity, fields, block_len), slots_dev
    )
    tiles = grid.reshape(faces, rows, fields, block_len)
    pick = jnp.eye(block_len, dtype=BF)[jnp.array([0, block_len - 1])]
    ends = jnp.einsum("ep,tcp->etc", pick, grid, preferred_element_type=F32).astype(BF)
    ends = ends.reshape(2, faces, rows, fields)
    spare = ((0, 0), (0, 0), (0, block_len - fields))
    lines = [
        jnp.pad(tiles[:, 0].transpose(0, 2, 1), spare),
        jnp.pad(tiles[:, -1].transpose(0, 2, 1), spare),
        jnp.pad(ends[0], spare),
        jnp.pad(ends[1], spare),
    ]
    halos = halo_exchange(lines, seam_table, rows, block_len, "halo1")
    hidden, ends = conv(True, grid, halos, conv1_weight, conv1_bias, faces, rows, block_len)
    tiles = hidden.reshape(faces, rows, block_len, hidden.shape[2])
    halos = halo_exchange([tiles, ends], seam_table, rows, block_len, "halo2")
    return conv(False, hidden, halos, conv2_weight, conv2_bias, faces, rows, block_len)


def solution(mesh):
    return jax.shard_map(
        local,
        mesh=mesh,
        in_specs=(
            P(None, ("band", "tile")),
            P(("band", "tile"), None, None, None),
            P(("band", "tile"), None),
            P(("band", "tile"), None),
            P(),
            P(),
            P(),
            P(),
            P(),
        ),
        out_specs=P(None, None, "band", "tile"),
        check_vma=False,
    )
```
